512 devices in a mesh: dp: 128 (over y, z, core), tensor: 4 (over x).
Axes of the slice: x: 4, y: 4, z: 16, core: 2. Of those that a mesh axis runs over, the one named last changes fastest.
Arguments:
- acts: bfloat16 [8, 32768, 2048], P(None, 'dp', 'tensor'), may hold values from -24 to 24
- out_cot: bfloat16 [8, 32768, 1024], P(None, 'dp', 'tensor'), may hold values from -24 to 24
- emb_ids: int32 [32768], P(('dp', 'tensor')), may hold values from 0 to 8191
- emb_cot: bfloat16 [32768, 1024], P('dp', 'tensor'), may hold values from -24 to 24
- grad_w: float32 [8192, 2048], P(('dp', 'tensor')), may hold values from -6 to 6
- grad_e: float32 [8192, 1024], P(('dp', 'tensor')), may hold values from -6 to 6
Outputs:
- update_w: float32 [8192, 2048], P('dp', 'tensor')
- update_e: float32 [8192, 1024], P(('dp', 'tensor'))
The draws below stay inside these ranges and needn't reach their ends.
All inputs are finite; a program needn't handle non-finite values. Where the reference program divides by a largest or mean magnitude, that divisor is 1e-20 or more.
Results may differ from the reference program's by a relative error of at most 0.0003.
Values sent between devices are 32-bit elements; how exact they have to be, the bound alone decides.
A program may use at most 64 MiB of HBM per device.

```python
import math
import jax
import jax.numpy as jnp
import numpy as np
from jax import lax

D = 1024
INNER = 2048
HEAD = 64
LAYERS = 8
NS_ITERS = 4
VOCAB = 8192
TOKENS = 32768


def scaled_rows(key, layers, cols):
    keys = jax.random.split(key, 4)
    shape = (layers, TOKENS, cols)
    groups = cols // HEAD
    rise = jnp.sqrt(1.0 + 2.0 * jnp.arange(TOKENS, dtype=jnp.float32) / TOKENS)
    base = jnp.clip(jax.random.normal(keys[0], shape, jnp.float32), -4.0, 4.0)
    common = 0.6 * jnp.clip(jax.random.normal(keys[1], (layers, TOKENS, groups), jnp.float32), -4.0, 4.0)
    row_scale = jnp.exp(jax.random.uniform(keys[2], (layers, TOKENS), jnp.float32, math.log(0.3), math.log(3.0)))
    col_scale = jnp.exp(jax.random.uniform(keys[3], (layers, cols), jnp.float32, math.log(0.3), math.log(3.0)))
    mixed = base + jnp.repeat(common, HEAD, axis=2)
    value = row_scale[:, :, None] * rise[None, :, None] * col_scale[:, None, :] * mixed
    return jnp.clip(value, -24.0, 24.0)


def draw_acts(key, part):
    return scaled_rows(jax.random.fold_in(key, 11), LAYERS, INNER).astype(jnp.bfloat16)


def draw_out_cot(key, part):
    return scaled_rows(jax.random.fold_in(key, 12), LAYERS, D).astype(jnp.bfloat16)


def draw_emb_cot(key, part):
    return scaled_rows(jax.random.fold_in(key, 13), 1, D)[0].astype(jnp.bfloat16)


def with_ends(drawn, stream_key, low, largest):
    extent = drawn.shape
    spot = [jax.random.randint(jax.random.fold_in(stream_key, axis), (), 0, extent[axis]) for axis in range(len(extent))]
    drawn = drawn.at[tuple(spot)].set(low)
    longest = extent.index(max(extent))
    spot[longest] = (spot[longest] + 1) % extent[longest]
    return drawn.at[tuple(spot)].set(largest)


def block_levels(own_key, dims, cuts, low, top_value):
    def one(position, blocks):
        heights = jax.random.uniform(jax.random.fold_in(jax.random.fold_in(own_key, 6), position), (blocks,), jnp.float32, low / len(cuts), top_value / len(cuts))
        return jnp.repeat(jnp.exp(heights), dims[position] // blocks).reshape((-1,) + (1,) * (len(dims) - position - 1))

    level = one(*cuts[0])
    for cut in cuts[1:]:
        level = level * one(*cut)
    return level


def rank_bounds(count, lean):
    loads = [(1 << 20) // math.isqrt(rank ** lean) + 1 for rank in range(1, count + 1)]
    scale = 1 + sum(loads) // (1 << 30)
    return np.cumsum(np.array([max(1, weight // scale) for weight in loads]))


def ranked_ids(stream_key, extent, count, lean):
    listing = rank_bounds(count, lean)
    ticket = jax.random.randint(jax.random.fold_in(stream_key, 1), extent, 0, int(listing[count - 1]))
    grade = jnp.searchsorted(jnp.asarray(listing, jnp.int32), ticket, side="right")
    return jax.random.permutation(jax.random.fold_in(stream_key, 2), count)[grade].astype(jnp.int32)


def noise(stream_key, shape, width, most, cuts=(), held_as=jnp.bfloat16):
    level = block_levels(stream_key, shape, cuts, -0.22, 0.18) if cuts else 1.0
    array = jax.random.normal(stream_key, shape, jnp.float32) * width * level
    return jnp.minimum(jnp.maximum(array, -most), most).astype(held_as)


def setup_inputs(seed: int = 0) -> dict:
    arg_keys = jax.random.split(jax.random.key(seed), 7)
    acts = draw_acts(jax.random.fold_in(arg_keys[6], 71), 0)
    out_cot = draw_out_cot(jax.random.fold_in(arg_keys[6], 71), 0)
    emb_ids = with_ends(ranked_ids(arg_keys[2], (TOKENS,), VOCAB, 2), jax.random.fold_in(arg_keys[2], 3), 0, VOCAB - 1).astype(jnp.int32)
    emb_cot = draw_emb_cot(jax.random.fold_in(arg_keys[6], 71), 0)
    grad_w = noise(arg_keys[4], (LAYERS * D, INNER), 1.0, 6.0, ((0, 512),), jnp.float32)
    grad_e = noise(arg_keys[5], (VOCAB, D), 1.0, 6.0, ((0, 512),), jnp.float32)
    return dict(acts=acts, out_cot=out_cot, emb_ids=emb_ids, emb_cot=emb_cot, grad_w=grad_w, grad_e=grad_e)


damp_root = 0.7

def newton_inverse(matrices):
    size = matrices.shape[-1]
    eye = jnp.eye(size, dtype=jnp.float32)
    bound = lax.optimization_barrier(jnp.max(lax.optimization_barrier(jnp.sum(jnp.abs(matrices), axis=-1)), axis=-1))
    approx = eye[None] / bound[:, None, None]
    for sweep in range(NS_ITERS):
        image = jnp.einsum('bij,bjk->bik', matrices, approx, precision=lax.Precision.HIGHEST)
        approx = jnp.einsum('bij,bjk->bik', approx, 2.0 * eye[None] - image, precision=lax.Precision.HIGHEST)
    return approx

def reference(acts, out_cot, emb_ids, emb_cot, grad_w, grad_e):
    heads = INNER // HEAD
    groups = D // HEAD

    def layer_grams(pair):
        inputs, grads = pair
        split_in = inputs.astype(jnp.float32).reshape(TOKENS, heads, HEAD)
        split_gr = grads.astype(jnp.float32).reshape(TOKENS, groups, HEAD)
        first = jnp.einsum('thi,thj->hij', split_in, split_in, precision=lax.Precision.HIGHEST)
        second = jnp.einsum('thi,thj->hij', split_gr, split_gr, precision=lax.Precision.HIGHEST)
        return (first, second)
    gram_a, gram_g = lax.map(layer_grams, (acts, out_cot))
    split_emb = emb_cot.astype(jnp.float32).reshape(TOKENS, groups, HEAD)
    gram_e = jnp.einsum('thi,thj->hij', split_emb, split_emb, precision=lax.Precision.HIGHEST)
    trace_a = lax.optimization_barrier(jnp.sum(jnp.trace(gram_a, axis1=2, axis2=3), axis=1))
    trace_g = lax.optimization_barrier(jnp.sum(jnp.trace(gram_g, axis1=2, axis2=3), axis=1))
    trace_e = jnp.sum(jnp.trace(gram_e, axis1=1, axis2=2))
    counts = jnp.zeros((VOCAB,), jnp.float32).at[emb_ids].add(1.0)
    ratio = jnp.sqrt(trace_a / (TOKENS * INNER) / (trace_g / (TOKENS * D)))
    ratio_e = jnp.sqrt(TOKENS / VOCAB / (trace_e / (TOKENS * D)))
    eye = jnp.eye(HEAD, dtype=jnp.float32)
    fac_a = gram_a / TOKENS + (damp_root * ratio)[:, None, None, None] * eye
    fac_g = gram_g / TOKENS + (damp_root / ratio)[:, None, None, None] * eye
    fac_e = gram_e / TOKENS + damp_root / ratio_e * eye
    row_scale = counts + damp_root * ratio_e
    inv_a = newton_inverse(fac_a.reshape(-1, HEAD, HEAD)).reshape(LAYERS, heads, HEAD, HEAD)
    inv_g = newton_inverse(fac_g.reshape(-1, HEAD, HEAD)).reshape(LAYERS, groups, HEAD, HEAD)
    inv_e = newton_inverse(fac_e)
    grad_view = grad_w.reshape(LAYERS, groups, HEAD, heads, HEAD)
    left = jnp.einsum('lgij,lgjhc->lgihc', inv_g, grad_view, precision=lax.Precision.HIGHEST)
    right = jnp.einsum('lgihc,lhcd->lgihd', left, inv_a, precision=lax.Precision.HIGHEST)
    update_w = right.reshape(LAYERS * D, INNER)
    scaled = jnp.einsum('rgi,gij->rgj', grad_e.reshape(VOCAB, groups, HEAD), inv_e, precision=lax.Precision.HIGHEST)
    update_e = scaled.reshape(VOCAB, D) / row_scale[:, None]
    return (update_w, update_e)
```

```python
import jax
import jax.numpy as jnp
from jax import lax
from jax.experimental import pallas as pl
from jax.experimental.pallas import tpu as pltpu
from jax.sharding import PartitionSpec as P

HEAD = 64
NS_ITERS = 4
DAMP = 0.7
LAYERS = 8
TOKENS = 32768
VOCAB = 8192
WIDTH = 1024
INNER = 2048
NX, NY, NZ = 4, 4, 16
MESH = pl.DeviceIdType.MESH
F32 = jnp.float32
HI = lax.Precision.HIGHEST
HOLD = (2, 5, 0)


def coords():
    d = lax.axis_index("dp").astype(jnp.int32)
    x = lax.axis_index("tensor").astype(jnp.int32)
    c = lax.rem(d, 2)
    z = lax.rem(lax.div(d, 2), NZ)
    y = lax.div(d, 2 * NZ)
    return x, y, z, c


def dev(x, y, z, c):
    return ((y * NZ + z) * 2 + c, x)


def send(src, dst, send_sem, recv_sem, device):
    return pltpu.make_async_remote_copy(
        src_ref=src, dst_ref=dst, send_sem=send_sem, recv_sem=recv_sem, device_id=device, device_id_type=MESH
    )


def loop(low, high, body):
    def step(k, carry):
        body(k)
        return carry

    lax.fori_loop(low, high, step, 0)


def pair_of(product):
    lane = lax.broadcasted_iota(jnp.int32, (HEAD, 2 * HEAD), 1)
    return jnp.where(lane < HEAD, product[:HEAD], product[HEAD:])


def blockdiag(pair):
    lane = lax.broadcasted_iota(jnp.int32, (HEAD, 2 * HEAD), 1)
    zero = jnp.zeros_like(pair)
    return jnp.concatenate([jnp.where(lane < HEAD, pair, zero), jnp.where(lane < HEAD, zero, pair)], axis=0)


def gram_kernel(acts, cot, emb, ids_row, ids_col, blk, eblk, m):
    lane = lax.broadcasted_iota(jnp.int32, (HEAD, 2 * HEAD), 1)
    row = lax.broadcasted_iota(jnp.int32, (HEAD, 2 * HEAD), 0)
    on_diag = (lane == row) | (lane == row + HEAD)

    def gram(x):
        full = lax.dot_general(x, x, (((0,), (0,)), ((), ())), preferred_element_type=F32)
        pair = pair_of(full)
        return pair, jnp.sum(jnp.where(on_diag, pair, 0.0), axis=0, keepdims=True)

    ids_r = ids_row[...]
    ids_c = ids_col[...]
    hit_row = (lax.broadcasted_iota(jnp.int32, (64, 64), 0) == lax.shift_right_logical(ids_r, 7)).astype(F32)
    hit_lane = (lax.broadcasted_iota(jnp.int32, (64, 128), 1) == (ids_c & 127)).astype(F32)
    hist = jnp.dot(hit_row.astype(jnp.bfloat16), hit_lane.astype(jnp.bfloat16), preferred_element_type=F32)
    sum_e = jnp.zeros((1, 128), F32)
    for core in range(2):
        pair, diag = gram(emb[:, 128 * core : 128 * core + 128])
        eblk[core] = pair
        sum_e = sum_e + diag
    rows = {}
    for layer in range(LAYERS):
        sum_a = jnp.zeros((1, 128), F32)
        sum_g = jnp.zeros((1, 128), F32)
        for core in range(2):
            for p in range(2):
                q = 2 * core + p
                pair, diag = gram(acts[layer, :, 128 * q : 128 * q + 128])
                blk[core, 3 * layer + p] = pair
                sum_a = sum_a + diag
            pair, diag = gram(cot[layer, :, 128 * core : 128 * core + 128])
            blk[core, 3 * layer + 2] = pair
            sum_g = sum_g + diag
        rows[layer] = (sum_a, sum_g)
    for y in range(NY):
        m[y, 0:16] = hist[16 * y : 16 * y + 16]
        tail = [rows[2 * y][0], rows[2 * y + 1][0], rows[2 * y][1], rows[2 * y + 1][1], sum_e]
        m[y, 16:24] = jnp.concatenate(tail + [jnp.zeros((3, 128), F32)], axis=0)


def reduce_kernel(
    blk, eblk, m, gw, own_o, e_o, tr_o, tile_o,
    rblk, reb, rm, s1, se, ms, nz, ec, ef, s2, ry, re, rmm, rey, rz, rn, eag, rt,
    c_s, c_r, y_s, y_r, e_s, e_r, m_s, m_r, ey_s, ey_r, z_s, z_r, n_s, n_r, g_s, g_r, t_s, t_r,
):
    x, y, z, c = coords()
    h = lax.div(z, 8)
    other = dev(x, y, z, 1 - c)

    def at_xy(k):
        return lax.rem(x + lax.div(k, 4), 4), lax.rem(y + lax.rem(k, 4), 4)

    def at_z(k):
        return dev(x, y, lax.rem(z + k, NZ), c)

    def at_y(k):
        return dev(x, lax.rem(y + k, NY), z, c)

    def at_x(k):
        return dev(lax.rem(x + k, NX), y, z, c)

    barrier = pltpu.get_barrier_semaphore()
    pl.semaphore_signal(barrier, inc=1, device_id=other, device_id_type=MESH)

    def greet_xy(k):
        xx, yy = at_xy(k)
        pl.semaphore_signal(barrier, inc=1, device_id=dev(xx, yy, z, c), device_id_type=MESH)

    def greet_z(k):
        pl.semaphore_signal(barrier, inc=1, device_id=at_z(k), device_id_type=MESH)

    loop(1, 16, greet_xy)
    loop(1, 16, greet_z)
    pl.semaphore_wait(barrier, 31)

    def core_chunk(i):
        k = (2, 1, 3, 0)[i]
        yy = lax.rem(y + k, NY)
        part = pl.ds(6 * yy, 6)
        return send(blk.at[1 - c, part], rblk.at[part], c_s.at[i], c_r.at[i], other)

    e_core = send(eblk.at[1 - c], reb, c_s.at[4], c_r.at[4], other)
    m_core = send(m, rm, c_s.at[5], c_r.at[5], other)
    e_core.start()
    m_core.start()
    for i in range(4):
        core_chunk(i).start()

    def g_copy(k):
        cols = pl.ds(pl.multiple_of(lax.rem(x + k, NX) * 512, 512), 512)
        return send(gw.at[:, cols], rt.at[k], t_s.at[k], t_r.at[k], at_x(k))

    def g_start(k):
        g_copy(k).start()

    loop(1, NX, g_start)

    e_core.wait_recv()
    e_sum = eblk[c] + reb[...]
    for k in range(NZ):
        se[k] = e_sum[4 * k : 4 * k + 4]

    def e_copy(k):
        return send(se.at[lax.rem(z + k, NZ)], re.at[k], e_s.at[k], e_r.at[k], at_z(k))

    def e_start(k):
        e_copy(k).start()

    loop(1, NZ, e_start)
    m_core.wait_recv()
    for k in range(NY):
        ms[k] = m[k] + rm[k]

    def m_copy(k):
        xx, yy = at_xy(k)
        return send(ms.at[yy], rmm.at[k], m_s.at[k], m_r.at[k], dev(xx, yy, z, c))

    def m_start(k):
        m_copy(k).start()

    loop(1, 16, m_start)

    def y_copy(k):
        part = pl.ds(6 * lax.rem(y + k, NY), 6)
        return send(s1.at[part], ry.at[k], y_s.at[k], y_r.at[k], at_y(k))

    for i in range(4):
        k = (2, 1, 3, 0)[i]
        core_chunk(i).wait_recv()
        first = 6 * lax.rem(y + k, NY)

        def add(j, first=first):
            s1[first + j] = blk[c, first + j] + rblk[first + j]

        loop(0, 6, add)
        if k:
            y_copy(k).start()

    def e_add(k, total):
        e_copy(k).wait_recv()
        return total + re[k]

    ec[...] = lax.fori_loop(1, NZ, e_add, se[z])

    def ey_copy(k):
        return send(ec, rey.at[k], ey_s.at[k], ey_r.at[k], at_y(k))

    def ey_start(k):
        ey_copy(k).start()

    loop(1, NY, ey_start)

    def m_add(k, total):
        m_copy(k).wait_recv()
        return total + rmm[k]

    n = lax.fori_loop(1, 16, m_add, ms[y])
    for k in range(NZ):
        nz[k] = jnp.concatenate([n[k : k + 1], n[16:23]], axis=0)

    def n_copy(k):
        return send(nz.at[lax.rem(z + k, NZ)], rn.at[k], n_s.at[k], n_r.at[k], at_z(k))

    def n_start(k):
        n_copy(k).start()

    loop(1, NZ, n_start)

    def ey_add(k, total):
        ey_copy(k).wait_recv()
        return total + rey[k]

    ef[...] = lax.fori_loop(1, NY, ey_add, ec[...])

    def g_out(k):
        return send(ef, eag.at[k], g_s.at[k], g_r.at[k], at_z(k))

    def g_out_start(k):
        g_out(k).start()

    loop(1, NZ, g_out_start)

    base = 6 * y
    for k in range(1, NY):
        y_copy(k).wait_recv()

    def z_copy(j):
        hold = 8 * (j // 3) + lax.rem(2 * x + c + HOLD[j % 3], 8)
        k = lax.rem(hold - z + NZ, NZ)
        return k, send(s2.at[j], rz.at[k], z_s.at[j], z_r.at[k], dev(x, y, hold, c))

    for j in range(6):
        s2[j] = (s1[base + j] + ry[1, j]) + (ry[2, j] + ry[3, j])
        k, copy = z_copy(j)

        @pl.when(k != 0)
        def _(copy=copy):
            copy.start()

    def n_add(k, total):
        n_copy(k).wait_recv()
        return total + rn[k]

    tr_o[...] = lax.fori_loop(1, NZ, n_add, nz[z])
    loop(1, NX, lambda k: g_copy(k).wait_recv())

    def tile_put(k):
        tile_o[lax.rem(x - k + NX, NX)] = rt[k]

    loop(1, NX, tile_put)
    tile_o[x] = gw[:, pl.ds(pl.multiple_of(x * 512, 512), 512)]

    loop(1, NZ, lambda k: g_out(k).wait_recv())

    def e_put(k):
        e_o[lax.rem(z - k + NZ, NZ)] = eag[k]

    loop(1, NZ, e_put)
    e_o[z] = ef[...]

    r = lax.rem(lax.rem(z, 8) - 2 * x - c + 16, 8)
    own_o[...] = s2[0]
    for p in range(3):

        @pl.when(r == HOLD[p])
        def _(p=p):
            def z_add(k, total):
                send(s2.at[0], rz.at[k], z_s.at[0], z_r.at[k], other).wait_recv()
                return total + rz[k]

            own_o[...] = lax.fori_loop(1, NZ, z_add, s2[3 * h + p])

    e_core.wait_send()
    m_core.wait_send()
    for i in range(4):
        core_chunk(i).wait_send()
    loop(1, NX, lambda k: g_copy(k).wait_send())
    loop(1, NZ, lambda k: e_copy(k).wait_send())
    loop(1, 16, lambda k: m_copy(k).wait_send())
    loop(1, NY, lambda k: y_copy(k).wait_send())
    loop(1, NY, lambda k: ey_copy(k).wait_send())
    loop(1, NZ, lambda k: n_copy(k).wait_send())
    loop(1, NZ, lambda k: g_out(k).wait_send())
    for j in range(6):
        k, copy = z_copy(j)

        @pl.when(k != 0)
        def _(copy=copy):
            copy.wait_send()


def trace_sums(tr):
    return jnp.sum(tr, axis=1, keepdims=True)


def inverse_kernel(own, e, tr, inv_own, inv_e):
    x, y, z, c = coords()
    sums = trace_sums(tr[...])
    low = z < 8
    ta = jnp.where(low, sums[1:2], sums[2:3])
    tg = jnp.where(low, sums[3:4], sums[4:5])
    ratio = jnp.sqrt((ta / (TOKENS * INNER)) / (tg / (TOKENS * WIDTH)))
    ratio_e = jnp.sqrt((TOKENS / VOCAB) / (sums[5:6] / (TOKENS * WIDTH)))
    is_g = lax.rem(lax.rem(z, 8) - 2 * x - c + 16, 8) == HOLD[2]
    shift = jnp.where(is_g, DAMP / ratio, DAMP * ratio)
    side = 2 * HEAD
    row = lax.broadcasted_iota(jnp.int32, (side, side), 0)
    lane = lax.broadcasted_iota(jnp.int32, (side, side), 1)
    eye = (row == lane).astype(F32)
    top = lax.broadcasted_iota(jnp.int32, (side, 1), 0) < HEAD

    def start(pair, amount):
        mat = blockdiag(pair) * (1.0 / TOKENS) + amount * eye
        sums = jnp.sum(jnp.abs(mat), axis=1, keepdims=True)
        bound = jnp.where(
            top,
            jnp.max(jnp.where(top, sums, 0.0), axis=0, keepdims=True),
            jnp.max(jnp.where(top, 0.0, sums), axis=0, keepdims=True),
        )
        return mat, eye / bound

    def fold(mat):
        return mat[:HEAD] + mat[HEAD:]

    m1, a1 = start(own[...], shift)
    m2, a2 = start(e[...], DAMP / ratio_e)
    for _ in range(NS_ITERS):
        i1 = jnp.dot(m1, a1, precision=HI, preferred_element_type=F32)
        i2 = jnp.dot(m2, a2, precision=HI, preferred_element_type=F32)
        a1 = jnp.dot(a1, 2.0 * eye - i1, precision=HI, preferred_element_type=F32)
        a2 = jnp.dot(a2, 2.0 * eye - i2, precision=HI, preferred_element_type=F32)
    inv_own[...] = fold(a1)
    inv_e[...] = fold(a2)


def spread_kernel(io, ie, a_o, g_o, e_o, ra, rg, re, a_s, a_r, g_s, g_r, e_s, e_r):
    x, y, z, c = coords()
    h = lax.div(z, 8)
    z8 = lax.rem(z, 8)
    u = 2 * x + c
    w = 2 * z8 + c

    def plane(k):
        v = lax.rem(u + k, 8)
        return dev(lax.div(v, 2), y, z, lax.rem(v, 2))

    def group(k):
        v = lax.rem(w + k, 16)
        return dev(x, y, 8 * h + lax.div(v, 2), lax.rem(v, 2))

    barrier = pltpu.get_barrier_semaphore()

    def greet_x(k):
        xx = lax.rem(x + 1 + lax.div(k, 2), NX)
        pl.semaphore_signal(barrier, inc=1, device_id=dev(xx, y, z, lax.rem(k, 2)), device_id_type=MESH)

    def greet_group(k):
        pl.semaphore_signal(barrier, inc=1, device_id=group(k), device_id_type=MESH)

    loop(0, 6, greet_x)
    loop(1, 16, greet_group)
    pl.semaphore_wait(barrier, 21)

    r = lax.rem(z8 - u + 16, 8)

    def a_copy(k, q):
        return send(io, ra.at[q], a_s.at[k], a_r.at[q], group(k))

    def g_copy(k):
        return send(io, rg, g_s.at[k], g_r, plane(k))

    def e_copy(k):
        return send(ie, re.at[k], e_s.at[k], e_r.at[k], plane(k))

    for p in range(2):

        @pl.when(r == HOLD[p])
        def _(p=p):
            loop(1, 16, lambda k: a_copy(k, 2 * c + p).start())

    @pl.when(r == HOLD[2])
    def _():
        loop(1, 8, lambda k: g_copy(k).start())

    loop(1, 8, lambda k: e_copy(k).start())

    e_o[u] = ie[...]

    def e_take(k):
        e_copy(k).wait_recv()
        e_o[lax.rem(u - k + 8, 8)] = re[k]

    loop(1, 8, e_take)

    @pl.when(r != HOLD[2])
    def _():
        g_copy(1).wait_recv()
        g_o[...] = rg[...]

    @pl.when(r == HOLD[2])
    def _():
        g_o[...] = io[...]

    for q in range(4):
        mine = (c == q // 2) & (r == HOLD[q % 2])

        @pl.when(mine)
        def _(q=q):
            a_o[q] = io[...]

        @pl.when(jnp.logical_not(mine))
        def _(q=q):
            a_copy(1, q).wait_recv()
            a_o[q] = ra[q]

    for p in range(2):

        @pl.when(r == HOLD[p])
        def _(p=p):
            loop(1, 16, lambda k: a_copy(k, 2 * c + p).wait_send())

    @pl.when(r == HOLD[2])
    def _():
        loop(1, 8, lambda k: g_copy(k).wait_send())

    loop(1, 8, lambda k: e_copy(k).wait_send())


def update_kernel(a, g, e, tile, ge, tr, w_o, e_o):
    x, y, z, c = coords()
    pair = g[...]
    g_block = jnp.where(c == 0, pair[:, :HEAD], pair[:, HEAD:])
    left = jnp.dot(g_block, tile[...], precision=HI, preferred_element_type=F32)
    for q in range(4):
        cols = slice(128 * q, 128 * q + 128)
        w_o[:, cols] = jnp.dot(left[:, cols], blockdiag(a[q]), precision=HI, preferred_element_type=F32)
    stats = tr[...]
    sums = trace_sums(stats)
    ratio_e = jnp.sqrt((TOKENS / VOCAB) / (sums[5:6] / (TOKENS * WIDTH)))
    lane = lax.broadcasted_iota(jnp.int32, (16, 128), 1)
    row = lax.broadcasted_iota(jnp.int32, (16, 128), 0)
    picked = jnp.where(lane == row + (64 * c + 16 * x), jnp.broadcast_to(stats[0:1], (16, 128)), 0.0)
    row_scale = jnp.sum(picked, axis=1, keepdims=True) + DAMP * ratio_e
    for u in range(8):
        cols = slice(128 * u, 128 * u + 128)
        e_o[:, cols] = jnp.dot(ge[:, cols], blockdiag(e[u]), precision=HI, preferred_element_type=F32) / row_scale


def vmem(count):
    return [pl.BlockSpec(memory_space=pltpu.VMEM)] * count


def shape(*dims):
    return jax.ShapeDtypeStruct(dims, F32)


def local(acts, out_cot, emb_ids, emb_cot, grad_w, grad_e):
    blk, eblk, m = pl.pallas_call(
        gram_kernel,
        out_shape=(shape(2, 24, 64, 128), shape(2, 64, 128), shape(4, 24, 128)),
        in_specs=vmem(5),
        out_specs=tuple(vmem(3)),
        name="grams",
    )(acts, out_cot, emb_cot, emb_ids.reshape(1, 64), emb_ids.reshape(64, 1))
    dma = pltpu.SemaphoreType.DMA
    own, e, tr, tile = pl.pallas_call(
        reduce_kernel,
        out_shape=(shape(64, 128), shape(16, 4, 128), shape(8, 128), shape(4, 16, 512)),
        in_specs=vmem(4),
        out_specs=tuple(vmem(4)),
        scratch_shapes=[
            pltpu.VMEM((24, 64, 128), F32),
            pltpu.VMEM((64, 128), F32),
            pltpu.VMEM((4, 24, 128), F32),
            pltpu.VMEM((24, 64, 128), F32),
            pltpu.VMEM((16, 4, 128), F32),
            pltpu.VMEM((4, 24, 128), F32),
            pltpu.VMEM((16, 8, 128), F32),
            pltpu.VMEM((4, 128), F32),
            pltpu.VMEM((4, 128), F32),
            pltpu.VMEM((6, 64, 128), F32),
            pltpu.VMEM((4, 6, 64, 128), F32),
            pltpu.VMEM((16, 4, 128), F32),
            pltpu.VMEM((16, 24, 128), F32),
            pltpu.VMEM((4, 4, 128), F32),
            pltpu.VMEM((16, 64, 128), F32),
            pltpu.VMEM((16, 8, 128), F32),
            pltpu.VMEM((16, 4, 128), F32),
            pltpu.VMEM((4, 16, 512), F32),
        ]
        + [dma((n,)) for n in (6, 6, 4, 4, 16, 16, 16, 16, 4, 4, 6, 16, 16, 16, 16, 16, 4, 4)],
        compiler_params=pltpu.CompilerParams(collective_id=0, has_side_effects=True),
        name="reduce",
    )(blk, eblk, m, grad_w)
    inv_own, inv_e = pl.pallas_call(
        inverse_kernel,
        out_shape=(shape(64, 128), shape(64, 128)),
        in_specs=vmem(3),
        out_specs=tuple(vmem(2)),
        name="inverse",
    )(own, e.reshape(64, 128), tr)
    inv_a, inv_g, all_e = pl.pallas_call(
        spread_kernel,
        out_shape=(shape(4, 64, 128), shape(64, 128), shape(8, 64, 128)),
        in_specs=vmem(2),
        out_specs=tuple(vmem(3)),
        scratch_shapes=[
            pltpu.VMEM((4, 64, 128), F32),
            pltpu.VMEM((64, 128), F32),
            pltpu.VMEM((8, 64, 128), F32),
            dma((16,)), dma((4,)), dma((8,)), dma, dma((8,)), dma((8,)),
        ],
        compiler_params=pltpu.CompilerParams(collective_id=1, has_side_effects=True),
        name="spread",
    )(inv_own, inv_e)
    return pl.pallas_call(
        update_kernel,
        out_shape=(shape(64, 512), shape(16, 1024)),
        in_specs=vmem(6),
        out_specs=tuple(vmem(2)),
        name="update",
    )(inv_a, inv_g, all_e, tile.reshape(64, 512), grad_e, tr)


def solution(mesh):
    in_specs = (
        P(None, "dp", "tensor"),
        P(None, "dp", "tensor"),
        P(("dp", "tensor")),
        P("dp", "tensor"),
        P(("dp", "tensor"), None),
        P(("dp", "tensor"), None),
    )
    out_specs = (P("dp", "tensor"), P(("dp", "tensor"), None))
    return jax.shard_map(local, mesh=mesh, in_specs=in_specs, out_specs=out_specs, check_vma=False)
```

```python
import jax
import jax.numpy as jnp
from jax import lax
from jax.experimental import pallas as pl
from jax.experimental.pallas import tpu as pltpu
from jax.sharding import PartitionSpec as P

HEAD = 64
NS_ITERS = 4
DAMP = 0.7
LAYERS = 8
TOKENS = 32768
VOCAB = 8192
WIDTH = 1024
INNER = 2048
NX, NY, NZ = 4, 4, 16
MESH = pl.DeviceIdType.MESH
F32 = jnp.float32
HI = lax.Precision.HIGHEST


def coords():
    d = lax.axis_index("dp").astype(jnp.int32)
    x = lax.axis_index("tensor").astype(jnp.int32)
    c = lax.rem(d, 2)
    z = lax.rem(lax.div(d, 2), NZ)
    y = lax.div(d, 2 * NZ)
    return x, y, z, c


def dev(x, y, z, c):
    return ((y * NZ + z) * 2 + c, x)


def hold(x, c, p):
    u = 2 * x + c
    if p == 2:
        return u
    if p == 0:
        return 3 - c
    return jnp.where(c == 0, jnp.where(u == 4, 5, 4), jnp.where(u == 5, 4, 5))


def send(src, dst, send_sem, recv_sem, device):
    return pltpu.make_async_remote_copy(
        src_ref=src, dst_ref=dst, send_sem=send_sem, recv_sem=recv_sem, device_id=device, device_id_type=MESH
    )


def loop(low, high, body):
    def step(k, carry):
        body(k)
        return carry

    lax.fori_loop(low, high, step, 0)


def pair_of(product):
    lane = lax.broadcasted_iota(jnp.int32, (HEAD, 2 * HEAD), 1)
    return jnp.where(lane < HEAD, product[:HEAD], product[HEAD:])


def blockdiag(pair):
    lane = lax.broadcasted_iota(jnp.int32, (HEAD, 2 * HEAD), 1)
    zero = jnp.zeros_like(pair)
    return jnp.concatenate([jnp.where(lane < HEAD, pair, zero), jnp.where(lane < HEAD, zero, pair)], axis=0)


def grams(acts, cot, emb, ids_row, blk, eblk, m):
    lane = lax.broadcasted_iota(jnp.int32, (HEAD, 2 * HEAD), 1)
    row = lax.broadcasted_iota(jnp.int32, (HEAD, 2 * HEAD), 0)
    on_diag = (lane == row) | (lane == row + HEAD)

    def gram(x):
        full = lax.dot_general(x, x, (((0,), (0,)), ((), ())), preferred_element_type=F32)
        pair = pair_of(full)
        return pair, jnp.sum(jnp.where(on_diag, pair, 0.0), axis=0, keepdims=True)

    ids = ids_row[...]
    hit_row = (lax.broadcasted_iota(jnp.int32, (64, 64), 0) == lax.shift_right_logical(ids, 7)).astype(F32)
    hit_lane = (lax.broadcasted_iota(jnp.int32, (128, 64), 0) == (ids & 127)).astype(F32)
    hist = lax.dot_general(
        hit_row.astype(jnp.bfloat16),
        hit_lane.astype(jnp.bfloat16),
        (((1,), (1,)), ((), ())),
        preferred_element_type=F32,
    )
    sum_e = jnp.zeros((1, 128), F32)
    for core in range(2):
        pair, diag = gram(emb[:, 128 * core : 128 * core + 128])
        eblk[core] = pair
        sum_e = sum_e + diag
    rows = {}
    for layer in range(LAYERS):
        sum_a = jnp.zeros((1, 128), F32)
        sum_g = jnp.zeros((1, 128), F32)
        for core in range(2):
            for p in range(2):
                q = 2 * core + p
                pair, diag = gram(acts[layer, :, 128 * q : 128 * q + 128])
                blk[core, 3 * layer + p] = pair
                sum_a = sum_a + diag
            pair, diag = gram(cot[layer, :, 128 * core : 128 * core + 128])
            blk[core, 3 * layer + 2] = pair
            sum_g = sum_g + diag
        rows[layer] = (sum_a, sum_g)
    for y in range(NY):
        m[y, 0:16] = hist[16 * y : 16 * y + 16]
        tail = [rows[2 * y][0], rows[2 * y + 1][0], rows[2 * y][1], rows[2 * y + 1][1], sum_e]
        m[y, 16:24] = jnp.concatenate(tail + [jnp.zeros((3, 128), F32)], axis=0)


def trace_sums(tr):
    return jnp.sum(tr, axis=1, keepdims=True)


def inverses(own, e, tr):
    x, y, z, c = coords()
    sums = trace_sums(tr)
    low = z < 8
    ta = jnp.where(low, sums[1:2], sums[2:3])
    tg = jnp.where(low, sums[3:4], sums[4:5])
    ratio = jnp.sqrt((ta / (TOKENS * INNER)) / (tg / (TOKENS * WIDTH)))
    ratio_e = jnp.sqrt((TOKENS / VOCAB) / (sums[5:6] / (TOKENS * WIDTH)))
    is_g = lax.rem(z, 8) == hold(x, c, 2)
    shift = jnp.where(is_g, DAMP / ratio, DAMP * ratio)
    side = 2 * HEAD
    row = lax.broadcasted_iota(jnp.int32, (side, side), 0)
    lane = lax.broadcasted_iota(jnp.int32, (side, side), 1)
    eye = (row == lane).astype(F32)
    top = lax.broadcasted_iota(jnp.int32, (side, 1), 0) < HEAD

    def start(pair, amount):
        mat = blockdiag(pair) * (1.0 / TOKENS) + amount * eye
        sums = jnp.sum(jnp.abs(mat), axis=1, keepdims=True)
        bound = jnp.where(
            top,
            jnp.max(jnp.where(top, sums, 0.0), axis=0, keepdims=True),
            jnp.max(jnp.where(top, 0.0, sums), axis=0, keepdims=True),
        )
        return mat, eye / bound

    def fold(mat):
        return mat[:HEAD] + mat[HEAD:]

    m1, a1 = start(own, shift)
    m2, a2 = start(e, DAMP / ratio_e)
    for _ in range(NS_ITERS):
        i1 = jnp.dot(m1, a1, precision=HI, preferred_element_type=F32)
        i2 = jnp.dot(m2, a2, precision=HI, preferred_element_type=F32)
        a1 = jnp.dot(a1, 2.0 * eye - i1, precision=HI, preferred_element_type=F32)
        a2 = jnp.dot(a2, 2.0 * eye - i2, precision=HI, preferred_element_type=F32)
    return fold(a1), fold(a2)


def whole_kernel(
    acts, cot, emb, ids_row, gw, ge, w_o, u_o,
    blk, eblk, m, own_v, e_v, tr_v,
    rblk, reb, rm, s1, se, ms, nz, ec, ef, s2, ry, re, rmm, rey, rz, rn, eag, rt,
    io, ie, ra, rg, ree,
    c_s, c_r, y_s, y_r, e_s, e_r, m_s, m_r, ey_s, ey_r, z_s, z_r, n_s, n_r, g_s, g_r, t_s, t_r,
    a_s, a_r, f_s, ig_s, ig_r, ie_s, ie_r,
):
    x, y, z, c = coords()
    h = lax.div(z, 8)
    z8 = lax.rem(z, 8)
    u = 2 * x + c
    other = dev(x, y, z, 1 - c)

    def at_xy(k):
        return lax.rem(x + lax.div(k, 4), 4), lax.rem(y + lax.rem(k, 4), 4)

    def at_z(k):
        return dev(x, y, lax.rem(z + k, NZ), c)

    def at_y(k):
        return dev(x, lax.rem(y + k, NY), z, c)

    def at_x(k):
        return dev(lax.rem(x + k, NX), y, z, c)

    barrier = pltpu.get_barrier_semaphore()
    pl.semaphore_signal(barrier, inc=1, device_id=other, device_id_type=MESH)

    def greet_xy(k):
        xx, yy = at_xy(k)
        pl.semaphore_signal(barrier, inc=1, device_id=dev(xx, yy, z, c), device_id_type=MESH)

    def greet_z(k):
        pl.semaphore_signal(barrier, inc=1, device_id=at_z(k), device_id_type=MESH)

    def greet_group(k):
        near = 8 * h + lax.rem(z8 + k, 8)
        pl.semaphore_signal(barrier, inc=1, device_id=dev(x, y, near, 1 - c), device_id_type=MESH)

    def greet_plane(k):
        pl.semaphore_signal(barrier, inc=1, device_id=dev(lax.rem(x + k, NX), y, z, 1 - c), device_id_type=MESH)

    loop(1, 16, greet_xy)
    loop(1, 16, greet_z)
    loop(1, 8, greet_group)
    loop(1, NX, greet_plane)
    grams(acts, cot, emb, ids_row, blk, eblk, m)
    pl.semaphore_wait(barrier, 41)

    def core_chunk(i):
        k = (2, 1, 3, 0)[i]
        yy = lax.rem(y + k, NY)
        part = pl.ds(6 * yy, 6)
        return send(blk.at[1 - c, part], rblk.at[part], c_s.at[i], c_r.at[i], other)

    e_core = send(eblk.at[1 - c], reb, c_s.at[4], c_r.at[4], other)
    m_core = send(m, rm, c_s.at[5], c_r.at[5], other)
    e_core.start()
    m_core.start()
    for i in range(4):
        core_chunk(i).start()

    def g_copy(k):
        cols = pl.ds(pl.multiple_of(lax.rem(x + k, NX) * 512, 512), 512)
        return send(gw.at[:, cols], rt.at[x], t_s.at[k], t_r.at[k], at_x(k))

    def g_start(k):
        g_copy(k).start()

    loop(1, NX, g_start)

    e_core.wait_recv()
    e_sum = eblk[c] + reb[...]
    for k in range(NZ):
        se[k] = e_sum[4 * k : 4 * k + 4]

    def e_copy(k):
        return send(se.at[lax.rem(z + k, NZ)], re.at[k], e_s.at[k], e_r.at[k], at_z(k))

    def e_start(k):
        e_copy(k).start()

    loop(1, NZ, e_start)
    m_core.wait_recv()
    for k in range(NY):
        ms[k] = m[k] + rm[k]

    def m_copy(k):
        xx, yy = at_xy(k)
        return send(ms.at[yy], rmm.at[k], m_s.at[k], m_r.at[k], dev(xx, yy, z, c))

    def m_start(k):
        m_copy(k).start()

    loop(1, 16, m_start)

    def y_copy(k):
        part = pl.ds(6 * lax.rem(y + k, NY), 6)
        return send(s1.at[part], ry.at[k], y_s.at[k], y_r.at[k], at_y(k))

    for i in range(4):
        k = (2, 1, 3, 0)[i]
        core_chunk(i).wait_recv()
        first = 6 * lax.rem(y + k, NY)

        def add(j, first=first):
            s1[first + j] = blk[c, first + j] + rblk[first + j]

        loop(0, 6, add)
        if k:
            y_copy(k).start()

    def e_add(k, total):
        e_copy(k).wait_recv()
        return total + re[k]

    ec[...] = lax.fori_loop(1, NZ, e_add, se[z])

    def ey_copy(k):
        return send(ec, rey.at[k], ey_s.at[k], ey_r.at[k], at_y(k))

    def ey_start(k):
        ey_copy(k).start()

    loop(1, NY, ey_start)

    def m_add(k, total):
        m_copy(k).wait_recv()
        return total + rmm[k]

    n = lax.fori_loop(1, 16, m_add, ms[y])
    for k in range(NZ):
        nz[k] = jnp.concatenate([n[k : k + 1], n[16:23]], axis=0)

    def n_copy(k):
        return send(nz.at[lax.rem(z + k, NZ)], rn.at[k], n_s.at[k], n_r.at[k], at_z(k))

    def n_start(k):
        n_copy(k).start()

    loop(1, NZ, n_start)

    def ey_add(k, total):
        ey_copy(k).wait_recv()
        return total + rey[k]

    ef[...] = lax.fori_loop(1, NY, ey_add, ec[...])

    def g_out(k):
        return send(ef, eag.at[z], g_s.at[k], g_r.at[k], at_z(k))

    def g_out_start(k):
        g_out(k).start()

    loop(1, NZ, g_out_start)

    base = 6 * y
    for k in range(1, NY):
        y_copy(k).wait_recv()

    def z_copy(j):
        place = 8 * (j // 3) + hold(x, c, j % 3)
        k = lax.rem(place - z + NZ, NZ)
        return k, send(s2.at[j], rz.at[k], z_s.at[j], z_r.at[k], dev(x, y, place, c))

    for j in range(6):
        s2[j] = (s1[base + j] + ry[1, j]) + (ry[2, j] + ry[3, j])
        k, copy = z_copy(j)

        @pl.when(k != 0)
        def _(copy=copy):
            copy.start()

    def n_add(k, total):
        n_copy(k).wait_recv()
        return total + rn[k]

    tr_v[...] = lax.fori_loop(1, NZ, n_add, nz[z])
    loop(1, NZ, lambda k: g_out(k).wait_recv())
    eag[z] = ef[...]
    for k in range(NZ):
        e_v[4 * k : 4 * k + 4] = eag[k]

    own_v[...] = s2[0]
    for p in range(3):

        @pl.when(z8 == hold(x, c, p))
        def _(p=p):
            def z_add(k, total):
                send(s2.at[0], rz.at[k], z_s.at[0], z_r.at[k], other).wait_recv()
                return total + rz[k]

            own_v[...] = lax.fori_loop(1, NZ, z_add, s2[3 * h + p])

    inv_own, inv_e = inverses(own_v[...], e_v[...], tr_v[...])
    io[...] = inv_own
    ie[...] = inv_e

    def a_copy(k, q):
        near = 8 * h + lax.rem(z8 + k, 8)
        return send(io, ra.at[q], a_s.at[k], a_r.at[q], dev(x, y, near, lax.rem(q, 2)))

    def a_side(q):
        return send(io, ra.at[q], a_s.at[0], a_r.at[q], other)

    def a_pass(q):
        return send(ra.at[q], ra.at[q], f_s.at[q], a_r.at[q], other)

    def plane(k):
        v = lax.rem(u + k, 8)
        return dev(lax.div(v, 2), y, z, lax.rem(v, 2))

    def ig_copy(k):
        return send(io, rg, ig_s.at[k], ig_r, plane(k))

    def ie_copy(k):
        return send(ie, ree.at[u], ie_s.at[k], ie_r.at[k], plane(k))

    for p in range(2):

        @pl.when(z8 == hold(x, c, p))
        def _(p=p):
            loop(1, 8, lambda k: a_copy(k, 2 * c + p).start())
            a_side(2 * c + p).start()
            ra[2 * c + p] = inv_own

    @pl.when(z8 == hold(x, c, 2))
    def _():
        loop(1, 8, lambda k: ig_copy(k).start())
        rg[...] = inv_own

    loop(1, 8, lambda k: ie_copy(k).start())
    ree[u] = inv_e
    loop(1, NX, lambda k: g_copy(k).wait_recv())
    rt[x] = gw[:, pl.ds(pl.multiple_of(x * 512, 512), 512)]

    @pl.when(z8 != hold(x, c, 2))
    def _():
        ig_copy(1).wait_recv()

    pair = rg[...]
    g_block = jnp.where(c == 0, pair[:, :HEAD], pair[:, HEAD:])
    tile = jnp.concatenate([rt[k] for k in range(NX)], axis=0)
    left = jnp.dot(g_block, tile, precision=HI, preferred_element_type=F32)
    for q in range(4):
        here = z8 == hold(x, q // 2, q % 2)

        @pl.when(jnp.logical_not(here) & (c == q % 2))
        def _(q=q):
            a_side(q).wait_recv()
            a_pass(q).start()

    loop(1, 8, lambda k: ie_copy(k).wait_recv())
    stats = tr_v[...]
    ratio_e = jnp.sqrt((TOKENS / VOCAB) / (trace_sums(stats)[5:6] / (TOKENS * WIDTH)))
    lane = lax.broadcasted_iota(jnp.int32, (16, 128), 1)
    row = lax.broadcasted_iota(jnp.int32, (16, 128), 0)
    picked = jnp.where(lane == row + (64 * c + 16 * x), jnp.broadcast_to(stats[0:1], (16, 128)), 0.0)
    row_scale = jnp.sum(picked, axis=1, keepdims=True) + DAMP * ratio_e
    for v in range(8):
        cols = slice(128 * v, 128 * v + 128)
        u_o[:, cols] = jnp.dot(ge[:, cols], blockdiag(ree[v]), precision=HI, preferred_element_type=F32) / row_scale
    for q in range(4):
        here = z8 == hold(x, q // 2, q % 2)

        @pl.when((here & (c != q // 2)) | (jnp.logical_not(here) & (c != q % 2)))
        def _(q=q):
            a_side(q).wait_recv()

        cols = slice(128 * q, 128 * q + 128)
        w_o[:, cols] = jnp.dot(left[:, cols], blockdiag(ra[q]), precision=HI, preferred_element_type=F32)

    for p in range(2):

        @pl.when(z8 == hold(x, c, p))
        def _(p=p):
            loop(1, 8, lambda k: a_copy(k, 2 * c + p).wait_send())
            a_side(2 * c + p).wait_send()

    for q in range(4):
        here = z8 == hold(x, q // 2, q % 2)

        @pl.when(jnp.logical_not(here) & (c == q % 2))
        def _(q=q):
            a_pass(q).wait_send()

    @pl.when(z8 == hold(x, c, 2))
    def _():
        loop(1, 8, lambda k: ig_copy(k).wait_send())

    loop(1, 8, lambda k: ie_copy(k).wait_send())
    e_core.wait_send()
    m_core.wait_send()
    for i in range(4):
        core_chunk(i).wait_send()
    loop(1, NX, lambda k: g_copy(k).wait_send())
    loop(1, NZ, lambda k: e_copy(k).wait_send())
    loop(1, 16, lambda k: m_copy(k).wait_send())
    loop(1, NY, lambda k: y_copy(k).wait_send())
    loop(1, NY, lambda k: ey_copy(k).wait_send())
    loop(1, NZ, lambda k: n_copy(k).wait_send())
    loop(1, NZ, lambda k: g_out(k).wait_send())
    for j in range(6):
        k, copy = z_copy(j)

        @pl.when(k != 0)
        def _(copy=copy):
            copy.wait_send()


def vmem(count):
    return [pl.BlockSpec(memory_space=pltpu.VMEM)] * count


def shape(*dims):
    return jax.ShapeDtypeStruct(dims, F32)


def local(acts, out_cot, emb_ids, emb_cot, grad_w, grad_e):
    dma = pltpu.SemaphoreType.DMA
    buffers = [
        (2, 24, 64, 128), (2, 64, 128), (4, 24, 128), (64, 128), (64, 128), (8, 128),
        (24, 64, 128), (64, 128), (4, 24, 128), (24, 64, 128), (16, 4, 128), (4, 24, 128),
        (16, 8, 128), (4, 128), (4, 128), (6, 64, 128), (4, 6, 64, 128), (16, 4, 128),
        (16, 24, 128), (4, 4, 128), (16, 64, 128), (16, 8, 128), (16, 4, 128), (4, 16, 512),
        (64, 128), (64, 128), (4, 64, 128), (64, 128), (8, 64, 128),
    ]
    return pl.pallas_call(
        whole_kernel,
        out_shape=(shape(64, 512), shape(16, 1024)),
        in_specs=vmem(6),
        out_specs=tuple(vmem(2)),
        scratch_shapes=[pltpu.VMEM(dims, F32) for dims in buffers]
        + [dma((n,)) for n in (6, 6, 4, 4, 16, 16, 16, 16, 4, 4, 6, 16, 16, 16, 16, 16, 4, 4)]
        + [dma((8,)), dma((4,)), dma((4,)), dma((8,)), dma, dma((8,)), dma((8,))],
        compiler_params=pltpu.CompilerParams(collective_id=0, has_side_effects=True),
        name="whole",
    )(acts, out_cot, emb_cot, emb_ids.reshape(1, 64), grad_w, grad_e)


def solution(mesh):
    in_specs = (
        P(None, "dp", "tensor"),
        P(None, "dp", "tensor"),
        P(("dp", "tensor")),
        P("dp", "tensor"),
        P(("dp", "tensor"), None),
        P(("dp", "tensor"), None),
    )
    out_specs = (P("dp", "tensor"), P(("dp", "tensor"), None))
    return jax.shard_map(local, mesh=mesh, in_specs=in_specs, out_specs=out_specs, check_vma=False)
```

```python
import jax
import jax.numpy as jnp
from jax import lax
from jax.experimental import pallas as pl
from jax.experimental.pallas import tpu as pltpu
from jax.sharding import PartitionSpec as P

HEAD = 64
NS_ITERS = 4
DAMP = 0.7
LAYERS = 8
TOKENS = 32768
VOCAB = 8192
WIDTH = 1024
INNER = 2048
NX, NY, NZ = 4, 4, 16
MESH = pl.DeviceIdType.MESH
F32 = jnp.float32
HI = lax.Precision.HIGHEST


def coords():
    d = lax.axis_index("dp").astype(jnp.int32)
    x = lax.axis_index("tensor").astype(jnp.int32)
    c = lax.rem(d, 2)
    z = lax.rem(lax.div(d, 2), NZ)
    y = lax.div(d, 2 * NZ)
    return x, y, z, c


def dev(x, y, z, c):
    return ((y * NZ + z) * 2 + c, x)


def a_place(core):
    return 3 + core


def send(src, dst, send_sem, recv_sem, device):
    return pltpu.make_async_remote_copy(
        src_ref=src, dst_ref=dst, send_sem=send_sem, recv_sem=recv_sem, device_id=device, device_id_type=MESH
    )


def loop(low, high, body):
    def step(k, carry):
        body(k)
        return carry

    lax.fori_loop(low, high, step, 0)


def pair_of(product):
    lane = lax.broadcasted_iota(jnp.int32, (HEAD, 2 * HEAD), 1)
    return jnp.where(lane < HEAD, product[:HEAD], product[HEAD:])


def blockdiag(pair):
    lane = lax.broadcasted_iota(jnp.int32, (HEAD, 2 * HEAD), 1)
    zero = jnp.zeros_like(pair)
    return jnp.concatenate([jnp.where(lane < HEAD, pair, zero), jnp.where(lane < HEAD, zero, pair)], axis=0)


def grams(acts, cot, emb, ids_row, blk, eblk, m):
    lane = lax.broadcasted_iota(jnp.int32, (HEAD, 2 * HEAD), 1)
    row = lax.broadcasted_iota(jnp.int32, (HEAD, 2 * HEAD), 0)
    on_diag = (lane == row) | (lane == row + HEAD)

    def gram(x):
        full = lax.dot_general(x, x, (((0,), (0,)), ((), ())), preferred_element_type=F32)
        pair = pair_of(full)
        return pair, jnp.sum(jnp.where(on_diag, pair, 0.0), axis=0, keepdims=True)

    ids = ids_row[...]
    hit_row = (lax.broadcasted_iota(jnp.int32, (64, 64), 0) == lax.shift_right_logical(ids, 7)).astype(F32)
    hit_lane = (lax.broadcasted_iota(jnp.int32, (128, 64), 0) == (ids & 127)).astype(F32)
    hist = lax.dot_general(
        hit_row.astype(jnp.bfloat16),
        hit_lane.astype(jnp.bfloat16),
        (((1,), (1,)), ((), ())),
        preferred_element_type=F32,
    )
    sum_e = jnp.zeros((1, 128), F32)
    for core in range(2):
        pair, diag = gram(emb[:, 128 * core : 128 * core + 128])
        eblk[core] = pair
        sum_e = sum_e + diag
    rows = {}
    upper = row <= jnp.where(lane < HEAD, lane, lane - HEAD)
    below = {}
    for layer in range(LAYERS):
        y, odd = layer // 2, layer % 2
        sum_a = jnp.zeros((1, 128), F32)
        sum_g = jnp.zeros((1, 128), F32)
        for core in range(2):
            first, diag_first = gram(acts[layer, :, 256 * core : 256 * core + 128])
            second, diag_second = gram(acts[layer, :, 256 * core + 128 : 256 * core + 256])
            blk[core, y, 64 * odd : 64 * odd + 64] = jnp.where(upper, first, second)
            below[core, odd] = diag_second
            sum_a = sum_a + (diag_first + diag_second)
        first, diag_first = gram(cot[layer, :, 0:128])
        second, diag_second = gram(cot[layer, :, 128:256])
        blk[odd, y, 128:192] = jnp.where(upper, first, second)
        below[odd, 2] = diag_second
        sum_g = sum_g + (diag_first + diag_second)
        rows[layer] = (sum_a, sum_g)
        if odd:
            for core in range(2):
                diags = [below[core, 0], below[core, 1], below[core, 2], jnp.zeros((5, 128), F32)]
                blk[core, y, 192:200] = jnp.concatenate(diags, axis=0)
    for y in range(NY):
        m[y, 0:16] = hist[16 * y : 16 * y + 16]
        tail = [rows[2 * y][0], rows[2 * y + 1][0], rows[2 * y][1], rows[2 * y + 1][1], sum_e]
        m[y, 16:24] = jnp.concatenate(tail + [jnp.zeros((3, 128), F32)], axis=0)


def trace_sums(tr):
    return jnp.sum(tr, axis=1, keepdims=True)


def inverses(own, e, tr):
    x, y, z, c = coords()
    sums = trace_sums(tr)
    low = z < 8
    ta = jnp.where(low, sums[1:2], sums[2:3])
    tg = jnp.where(low, sums[3:4], sums[4:5])
    ratio = jnp.sqrt((ta / (TOKENS * INNER)) / (tg / (TOKENS * WIDTH)))
    ratio_e = jnp.sqrt((TOKENS / VOCAB) / (sums[5:6] / (TOKENS * WIDTH)))
    is_g = lax.rem(z, 8) == 2 * x + c
    shift = jnp.where(is_g, DAMP / ratio, DAMP * ratio)
    side = 2 * HEAD
    row = lax.broadcasted_iota(jnp.int32, (side, side), 0)
    lane = lax.broadcasted_iota(jnp.int32, (side, side), 1)
    eye = (row == lane).astype(F32)
    top = lax.broadcasted_iota(jnp.int32, (side, 1), 0) < HEAD

    def start(pair, amount):
        mat = blockdiag(pair) * (1.0 / TOKENS) + amount * eye
        sums = jnp.sum(jnp.abs(mat), axis=1, keepdims=True)
        bound = jnp.where(
            top,
            jnp.max(jnp.where(top, sums, 0.0), axis=0, keepdims=True),
            jnp.max(jnp.where(top, 0.0, sums), axis=0, keepdims=True),
        )
        return mat, eye / bound

    def fold(mat):
        return mat[:HEAD] + mat[HEAD:]

    both = own[:HEAD]
    turned = fold(blockdiag(both).T)
    at = lax.broadcasted_iota(jnp.int32, (HEAD, side), 0)
    to = lax.broadcasted_iota(jnp.int32, (HEAD, side), 1)
    to = jnp.where(to < HEAD, to, to - HEAD)
    first = jnp.where(at <= to, both, turned)
    second = jnp.where(at > to, both, jnp.where(at == to, own[HEAD : HEAD + 1], turned))
    m0, a0 = start(first, shift)
    m1, a1 = start(second, shift)
    m2, a2 = start(e, DAMP / ratio_e)
    for _ in range(NS_ITERS):
        i0 = jnp.dot(m0, a0, precision=HI, preferred_element_type=F32)
        i1 = jnp.dot(m1, a1, precision=HI, preferred_element_type=F32)
        i2 = jnp.dot(m2, a2, precision=HI, preferred_element_type=F32)
        a0 = jnp.dot(a0, 2.0 * eye - i0, precision=HI, preferred_element_type=F32)
        a1 = jnp.dot(a1, 2.0 * eye - i1, precision=HI, preferred_element_type=F32)
        a2 = jnp.dot(a2, 2.0 * eye - i2, precision=HI, preferred_element_type=F32)
    return fold(a0), fold(a1), fold(a2)


def whole_kernel(
    acts, cot, emb, ids_row, gw, ge, w_o, u_o,
    blk, eblk, m, own_v, e_v, tr_v,
    rblk, reb, rm, s1, se, ms, nz, ec, ef, s2, ry, re, rmm, rey, rz, rn, eag, rt,
    ia, ib, ie, ra, rg, ree,
    c_s, c_r, y_s, y_r, e_s, e_r, m_s, m_r, ey_s, ey_r, z_s, z_r, n_s, n_r, g_s, g_r, t_s, t_r,
    a_s, a_r, f_s, ig_s, ig_r, ie_s, ie_r,
):
    x, y, z, c = coords()
    h = lax.div(z, 8)
    z8 = lax.rem(z, 8)
    u = 2 * x + c
    z_near = z + 1 - 2 * lax.rem(z, 2)
    is_a = z8 == a_place(c)
    is_g = (z8 == u) & (h == c)
    other = dev(x, y, z, 1 - c)

    def at_xy(k):
        return lax.rem(x + lax.div(k, 4), 4), lax.rem(y + lax.rem(k, 4), 4)

    def at_z(k):
        return dev(x, y, lax.rem(z + k, NZ), c)

    def at_y(k):
        return dev(x, lax.rem(y + k, NY), z, c)

    def at_x(k):
        return dev(lax.rem(x + k, NX), y, z, c)

    barrier = pltpu.get_barrier_semaphore()
    pl.semaphore_signal(barrier, inc=1, device_id=other, device_id_type=MESH)

    def greet_xy(k):
        xx, yy = at_xy(k)
        pl.semaphore_signal(barrier, inc=1, device_id=dev(xx, yy, z, c), device_id_type=MESH)

    def greet_z(k):
        pl.semaphore_signal(barrier, inc=1, device_id=at_z(k), device_id_type=MESH)

    def greet_group(k):
        near = 8 * h + lax.rem(z8 + k, 8)
        pl.semaphore_signal(barrier, inc=1, device_id=dev(x, y, near, 1 - c), device_id_type=MESH)

    def greet_plane(k):
        pl.semaphore_signal(barrier, inc=1, device_id=dev(lax.rem(x + k, NX), y, z, 1 - c), device_id_type=MESH)

    loop(1, 16, greet_xy)
    loop(1, 16, greet_z)
    loop(1, 8, greet_group)
    def greet_near(k):
        xx = lax.rem(x + 1 + lax.div(k, 2), NX)
        pl.semaphore_signal(barrier, inc=1, device_id=dev(xx, y, z_near, lax.rem(k, 2)), device_id_type=MESH)

    loop(1, NX, greet_plane)
    loop(0, 6, greet_near)
    grams(acts, cot, emb, ids_row, blk, eblk, m)
    pl.semaphore_wait(barrier, 47)

    def core_chunk(i):
        k = (2, 1, 3, 0)[i]
        yy = lax.rem(y + k, NY)
        return send(blk.at[1 - c, yy], rblk.at[yy], c_s.at[i], c_r.at[i], other)

    e_core = send(eblk.at[1 - c], reb, c_s.at[4], c_r.at[4], other)
    m_core = send(m, rm, c_s.at[5], c_r.at[5], other)
    e_core.start()
    m_core.start()
    for i in range(4):
        core_chunk(i).start()

    def g_copy(k):
        cols = pl.ds(pl.multiple_of(lax.rem(x + k, NX) * 512, 512), 512)
        return send(gw.at[:, cols], rt.at[x], t_s.at[k], t_r.at[k], at_x(k))

    def g_start(k):
        g_copy(k).start()

    loop(1, NX, g_start)

    e_core.wait_recv()
    e_sum = eblk[c] + reb[...]
    for k in range(NZ):
        se[k] = e_sum[4 * k : 4 * k + 4]

    def e_copy(k):
        return send(se.at[lax.rem(z + k, NZ)], re.at[k], e_s.at[k], e_r.at[k], at_z(k))

    def e_start(k):
        e_copy(k).start()

    loop(1, NZ, e_start)
    m_core.wait_recv()
    for k in range(NY):
        ms[k] = m[k] + rm[k]

    def m_copy(k):
        xx, yy = at_xy(k)
        return send(ms.at[yy], rmm.at[k], m_s.at[k], m_r.at[k], dev(xx, yy, z, c))

    def m_start(k):
        m_copy(k).start()

    loop(1, 16, m_start)

    def y_copy(k):
        return send(s1.at[lax.rem(y + k, NY)], ry.at[k], y_s.at[k], y_r.at[k], at_y(k))

    for i in range(4):
        k = (2, 1, 3, 0)[i]
        core_chunk(i).wait_recv()
        yy = lax.rem(y + k, NY)
        s1[yy] = blk[c, yy] + rblk[yy]
        if k:
            y_copy(k).start()

    def e_add(k, total):
        e_copy(k).wait_recv()
        return total + re[k]

    ec[...] = lax.fori_loop(1, NZ, e_add, se[z])

    def ey_copy(k):
        return send(ec, rey.at[k], ey_s.at[k], ey_r.at[k], at_y(k))

    def ey_start(k):
        ey_copy(k).start()

    loop(1, NY, ey_start)

    def m_add(k, total):
        m_copy(k).wait_recv()
        return total + rmm[k]

    n = lax.fori_loop(1, 16, m_add, ms[y])
    for k in range(NZ):
        nz[k] = jnp.concatenate([n[k : k + 1], n[16:23]], axis=0)

    def n_copy(k):
        return send(nz.at[lax.rem(z + k, NZ)], rn.at[k], n_s.at[k], n_r.at[k], at_z(k))

    def n_start(k):
        n_copy(k).start()

    loop(1, NZ, n_start)

    def ey_add(k, total):
        ey_copy(k).wait_recv()
        return total + rey[k]

    ef[...] = lax.fori_loop(1, NY, ey_add, ec[...])

    def g_out(k):
        return send(ef, eag.at[z], g_s.at[k], g_r.at[k], at_z(k))

    def g_out_start(k):
        g_out(k).start()

    loop(1, NZ, g_out_start)

    for k in range(1, NY):
        y_copy(k).wait_recv()

    def z_copy(j):
        place = 8 * c + u if j == 2 else 8 * j + a_place(c)
        k = lax.rem(place - z + NZ, NZ)
        return k, send(s2.at[j], rz.at[k], z_s.at[j], z_r.at[k], dev(x, y, place, c))

    chunk = (s1[y] + ry[1]) + (ry[2] + ry[3])
    for j in range(3):
        s2[j, 0:64] = chunk[64 * j : 64 * j + 64]
        s2[j, 64:72] = jnp.broadcast_to(chunk[192 + j : 193 + j], (8, 128))
        k, copy = z_copy(j)

        @pl.when(k != 0)
        def _(copy=copy):
            copy.start()

    def n_add(k, total):
        n_copy(k).wait_recv()
        return total + rn[k]

    tr_v[...] = lax.fori_loop(1, NZ, n_add, nz[z])
    loop(1, NZ, lambda k: g_out(k).wait_recv())
    eag[z] = ef[...]
    for k in range(NZ):
        e_v[4 * k : 4 * k + 4] = eag[k]

    own_v[...] = s2[0]

    @pl.when(is_a | is_g)
    def _():
        def z_add(k, total):
            send(s2.at[0], rz.at[k], z_s.at[0], z_r.at[k], other).wait_recv()
            return total + rz[k]

        own_v[...] = lax.fori_loop(1, NZ, z_add, s2[jnp.where(is_a, h, 2)])

    ia[...], ib[...], ie[...] = inverses(own_v[...], e_v[...], tr_v[...])

    def a_copy(k, p):
        near = 8 * h + lax.rem(z8 + k, 8)
        return send((ia, ib)[p], ra.at[2 * c + p], a_s.at[8 * p + k], a_r.at[2 * c + p], dev(x, y, near, p))

    def a_side(p):
        return send((ia, ib)[p], ra.at[2 * c + p], a_s.at[8 * p], a_r.at[2 * c + p], other)

    def a_came(q):
        send(ia, ra.at[q], a_s.at[0], a_r.at[q], other).wait_recv()

    def a_pass(q):
        return send(ra.at[q], ra.at[q], f_s.at[q], a_r.at[q], other)

    def plane(k):
        v = lax.rem(u + k, 8)
        return dev(lax.div(v, 2), y, z, lax.rem(v, 2))

    def near_plane(k):
        return dev(lax.div(k, 2), y, z_near, lax.rem(k, 2))

    def ig_here(p, k):
        return send((ia, ib)[p], rg, ig_s.at[k], ig_r, plane(k))

    def ig_there(p, k):
        return send((ia, ib)[p], rg, ig_s.at[8 + k], ig_r, near_plane(k))

    def ie_copy(k):
        return send(ie, ree.at[u], ie_s.at[k], ie_r.at[k], plane(k))

    @pl.when(is_a)
    def _():
        for p in range(2):
            loop(1, 8, lambda k, p=p: a_copy(k, p).start())
        for p in range(2):
            a_side(p).start()
        ra[2 * c] = ia[...]
        ra[2 * c + 1] = ib[...]

    for p in range(2):

        @pl.when(is_g & (c == p))
        def _(p=p):
            loop(0, 8, lambda k: ig_there(1 - p, k).start())
            loop(1, 8, lambda k: ig_here(p, k).start())
            rg[...] = (ia, ib)[p][...]

    loop(1, 8, lambda k: ie_copy(k).start())
    ree[u] = ie[...]
    loop(1, NX, lambda k: g_copy(k).wait_recv())
    rt[x] = gw[:, pl.ds(pl.multiple_of(x * 512, 512), 512)]

    @pl.when(jnp.logical_not(is_g))
    def _():
        send(ia, rg, ig_s.at[0], ig_r, other).wait_recv()

    pair = rg[...]
    g_block = jnp.where(c == 0, pair[:, :HEAD], pair[:, HEAD:])
    tile = jnp.concatenate([rt[k] for k in range(NX)], axis=0)
    left = jnp.dot(g_block, tile, precision=HI, preferred_element_type=F32)
    for q in range(4):
        here = z8 == a_place(q // 2)

        @pl.when(jnp.logical_not(here) & (c == q % 2))
        def _(q=q):
            a_came(q)
            a_pass(q).start()

    loop(1, 8, lambda k: ie_copy(k).wait_recv())
    stats = tr_v[...]
    ratio_e = jnp.sqrt((TOKENS / VOCAB) / (trace_sums(stats)[5:6] / (TOKENS * WIDTH)))
    lane = lax.broadcasted_iota(jnp.int32, (16, 128), 1)
    row = lax.broadcasted_iota(jnp.int32, (16, 128), 0)
    picked = jnp.where(lane == row + (64 * c + 16 * x), jnp.broadcast_to(stats[0:1], (16, 128)), 0.0)
    row_scale = jnp.sum(picked, axis=1, keepdims=True) + DAMP * ratio_e
    for v in range(8):
        cols = slice(128 * v, 128 * v + 128)
        u_o[:, cols] = jnp.dot(ge[:, cols], blockdiag(ree[v]), precision=HI, preferred_element_type=F32) / row_scale
    for q in range(4):
        here = z8 == a_place(q // 2)

        @pl.when((here & (c != q // 2)) | (jnp.logical_not(here) & (c != q % 2)))
        def _(q=q):
            a_came(q)

        cols = slice(128 * q, 128 * q + 128)
        w_o[:, cols] = jnp.dot(left[:, cols], blockdiag(ra[q]), precision=HI, preferred_element_type=F32)

    @pl.when(is_a)
    def _():
        for p in range(2):
            loop(1, 8, lambda k, p=p: a_copy(k, p).wait_send())
            a_side(p).wait_send()

    for q in range(4):
        here = z8 == a_place(q // 2)

        @pl.when(jnp.logical_not(here) & (c == q % 2))
        def _(q=q):
            a_pass(q).wait_send()

    for p in range(2):

        @pl.when(is_g & (c == p))
        def _(p=p):
            loop(0, 8, lambda k: ig_there(1 - p, k).wait_send())
            loop(1, 8, lambda k: ig_here(p, k).wait_send())

    loop(1, 8, lambda k: ie_copy(k).wait_send())
    e_core.wait_send()
    m_core.wait_send()
    for i in range(4):
        core_chunk(i).wait_send()
    loop(1, NX, lambda k: g_copy(k).wait_send())
    loop(1, NZ, lambda k: e_copy(k).wait_send())
    loop(1, 16, lambda k: m_copy(k).wait_send())
    loop(1, NY, lambda k: y_copy(k).wait_send())
    loop(1, NY, lambda k: ey_copy(k).wait_send())
    loop(1, NZ, lambda k: n_copy(k).wait_send())
    loop(1, NZ, lambda k: g_out(k).wait_send())
    for j in range(3):
        k, copy = z_copy(j)

        @pl.when(k != 0)
        def _(copy=copy):
            copy.wait_send()


def vmem(count):
    return [pl.BlockSpec(memory_space=pltpu.VMEM)] * count


def shape(*dims):
    return jax.ShapeDtypeStruct(dims, F32)


def local(acts, out_cot, emb_ids, emb_cot, grad_w, grad_e):
    dma = pltpu.SemaphoreType.DMA
    buffers = [
        (2, 4, 200, 128), (2, 64, 128), (4, 24, 128), (72, 128), (64, 128), (8, 128),
        (4, 200, 128), (64, 128), (4, 24, 128), (4, 200, 128), (16, 4, 128), (4, 24, 128),
        (16, 8, 128), (4, 128), (4, 128), (3, 72, 128), (4, 200, 128), (16, 4, 128),
        (16, 24, 128), (4, 4, 128), (16, 72, 128), (16, 8, 128), (16, 4, 128), (4, 16, 512),
        (64, 128), (64, 128), (64, 128), (4, 64, 128), (64, 128), (8, 64, 128),
    ]
    return pl.pallas_call(
        whole_kernel,
        out_shape=(shape(64, 512), shape(16, 1024)),
        in_specs=vmem(6),
        out_specs=tuple(vmem(2)),
        scratch_shapes=[pltpu.VMEM(dims, F32) for dims in buffers]
        + [dma((n,)) for n in (6, 6, 4, 4, 16, 16, 16, 16, 4, 4, 6, 16, 16, 16, 16, 16, 4, 4)]
        + [dma((16,)), dma((4,)), dma((4,)), dma((16,)), dma, dma((8,)), dma((8,))],
        compiler_params=pltpu.CompilerParams(collective_id=0, has_side_effects=True),
        name="whole",
    )(acts, out_cot, emb_cot, emb_ids.reshape(1, 64), grad_w, grad_e)


def solution(mesh):
    in_specs = (
        P(None, "dp", "tensor"),
        P(None, "dp", "tensor"),
        P(("dp", "tensor")),
        P("dp", "tensor"),
        P(("dp", "tensor"), None),
        P(("dp", "tensor"), None),
    )
    out_specs = (P("dp", "tensor"), P(("dp", "tensor"), None))
    return jax.shard_map(local, mesh=mesh, in_specs=in_specs, out_specs=out_specs, check_vma=False)
```

```python
import jax
import jax.numpy as jnp
from jax import lax
from jax.experimental import pallas as pl
from jax.experimental.pallas import tpu as pltpu
from jax.sharding import PartitionSpec as P

HEAD = 64
NS_ITERS = 4
DAMP = 0.7
LAYERS = 8
TOKENS = 32768
VOCAB = 8192
WIDTH = 1024
INNER = 2048
NX, NY, NZ = 4, 4, 16
MESH = pl.DeviceIdType.MESH
F32 = jnp.float32
HI = lax.Precision.HIGHEST


def coords():
    d = lax.axis_index("dp").astype(jnp.int32)
    x = lax.axis_index("tensor").astype(jnp.int32)
    c = lax.rem(d, 2)
    z = lax.rem(lax.div(d, 2), NZ)
    y = lax.div(d, 2 * NZ)
    return x, y, z, c


def dev(x, y, z, c):
    return ((y * NZ + z) * 2 + c, x)


def a_place(core):
    return 3 + core


def send(src, dst, send_sem, recv_sem, device):
    return pltpu.make_async_remote_copy(
        src_ref=src, dst_ref=dst, send_sem=send_sem, recv_sem=recv_sem, device_id=device, device_id_type=MESH
    )


def loop(low, high, body):
    def step(k, carry):
        body(k)
        return carry

    lax.fori_loop(low, high, step, 0)


def pair_of(product):
    lane = lax.broadcasted_iota(jnp.int32, (HEAD, 2 * HEAD), 1)
    return jnp.where(lane < HEAD, product[:HEAD], product[HEAD:])


def blockdiag(pair):
    lane = lax.broadcasted_iota(jnp.int32, (HEAD, 2 * HEAD), 1)
    zero = jnp.zeros_like(pair)
    return jnp.concatenate([jnp.where(lane < HEAD, pair, zero), jnp.where(lane < HEAD, zero, pair)], axis=0)


def grams(acts, cot, emb, ids_row, blk, eblk, m):
    lane = lax.broadcasted_iota(jnp.int32, (HEAD, 2 * HEAD), 1)
    row = lax.broadcasted_iota(jnp.int32, (HEAD, 2 * HEAD), 0)
    on_diag = (lane == row) | (lane == row + HEAD)

    def gram(x):
        full = lax.dot_general(x, x, (((0,), (0,)), ((), ())), preferred_element_type=F32)
        pair = pair_of(full)
        return pair, jnp.sum(jnp.where(on_diag, pair, 0.0), axis=0, keepdims=True)

    ids = ids_row[...]
    hit_row = (lax.broadcasted_iota(jnp.int32, (64, 64), 0) == lax.shift_right_logical(ids, 7)).astype(F32)
    hit_lane = (lax.broadcasted_iota(jnp.int32, (128, 64), 0) == (ids & 127)).astype(F32)
    hist = lax.dot_general(
        hit_row.astype(jnp.bfloat16),
        hit_lane.astype(jnp.bfloat16),
        (((1,), (1,)), ((), ())),
        preferred_element_type=F32,
    )
    sum_e = jnp.zeros((1, 128), F32)
    for core in range(2):
        pair, diag = gram(emb[:, 128 * core : 128 * core + 128])
        eblk[core] = pair
        sum_e = sum_e + diag
    rows = {}
    upper = row <= jnp.where(lane < HEAD, lane, lane - HEAD)
    below = {}
    for layer in range(LAYERS):
        y, odd = layer // 2, layer % 2
        sum_a = jnp.zeros((1, 128), F32)
        sum_g = jnp.zeros((1, 128), F32)
        for core in range(2):
            first, diag_first = gram(acts[layer, :, 256 * core : 256 * core + 128])
            second, diag_second = gram(acts[layer, :, 256 * core + 128 : 256 * core + 256])
            blk[core, y, 64 * odd : 64 * odd + 64] = jnp.where(upper, first, second)
            below[core, odd] = diag_second
            sum_a = sum_a + (diag_first + diag_second)
        first, diag_first = gram(cot[layer, :, 0:128])
        second, diag_second = gram(cot[layer, :, 128:256])
        blk[odd, y, 128:192] = jnp.where(upper, first, second)
        below[odd, 2] = diag_second
        sum_g = sum_g + (diag_first + diag_second)
        rows[layer] = (sum_a, sum_g)
        if odd:
            for core in range(2):
                diags = [below[core, 0], below[core, 1], below[core, 2], jnp.zeros((5, 128), F32)]
                blk[core, y, 192:200] = jnp.concatenate(diags, axis=0)
    for y in range(NY):
        m[y, 0:16] = hist[16 * y : 16 * y + 16]
        tail = [rows[2 * y][0], rows[2 * y + 1][0], rows[2 * y][1], rows[2 * y + 1][1], sum_e]
        m[y, 16:24] = jnp.concatenate(tail + [jnp.zeros((3, 128), F32)], axis=0)


def trace_sums(tr):
    return jnp.sum(tr, axis=1, keepdims=True)


def inverses(own, e, tr):
    x, y, z, c = coords()
    sums = trace_sums(tr)
    ta = sums[1:2]
    tg = sums[2:3]
    ratio = jnp.sqrt((ta / (TOKENS * INNER)) / (tg / (TOKENS * WIDTH)))
    ratio_e = jnp.sqrt((TOKENS / VOCAB) / (sums[3:4] / (TOKENS * WIDTH)))
    is_g = lax.rem(z, 8) == 2 * x + c
    shift = jnp.where(is_g, DAMP / ratio, DAMP * ratio)
    side = 2 * HEAD
    row = lax.broadcasted_iota(jnp.int32, (side, side), 0)
    lane = lax.broadcasted_iota(jnp.int32, (side, side), 1)
    eye = (row == lane).astype(F32)
    top = lax.broadcasted_iota(jnp.int32, (side, 1), 0) < HEAD

    def start(pair, amount):
        mat = blockdiag(pair) * (1.0 / TOKENS) + amount * eye
        sums = jnp.sum(jnp.abs(mat), axis=1, keepdims=True)
        bound = jnp.where(
            top,
            jnp.max(jnp.where(top, sums, 0.0), axis=0, keepdims=True),
            jnp.max(jnp.where(top, 0.0, sums), axis=0, keepdims=True),
        )
        return mat, eye / bound

    def fold(mat):
        return mat[:HEAD] + mat[HEAD:]

    both = own[:HEAD]
    turned = fold(blockdiag(both).T)
    at = lax.broadcasted_iota(jnp.int32, (HEAD, side), 0)
    to = lax.broadcasted_iota(jnp.int32, (HEAD, side), 1)
    to = jnp.where(to < HEAD, to, to - HEAD)
    first = jnp.where(at <= to, both, turned)
    second = jnp.where(at > to, both, jnp.where(at == to, own[HEAD : HEAD + 1], turned))
    m0, a0 = start(first, shift)
    m1, a1 = start(second, shift)
    m2, a2 = start(e, DAMP / ratio_e)
    for _ in range(NS_ITERS):
        i0 = jnp.dot(m0, a0, precision=HI, preferred_element_type=F32)
        i1 = jnp.dot(m1, a1, precision=HI, preferred_element_type=F32)
        i2 = jnp.dot(m2, a2, precision=HI, preferred_element_type=F32)
        a0 = jnp.dot(a0, 2.0 * eye - i0, precision=HI, preferred_element_type=F32)
        a1 = jnp.dot(a1, 2.0 * eye - i1, precision=HI, preferred_element_type=F32)
        a2 = jnp.dot(a2, 2.0 * eye - i2, precision=HI, preferred_element_type=F32)
    return fold(a0), fold(a1), fold(a2)


def whole_kernel(
    acts, cot, emb, ids_row, gw, ge, w_o, u_o,
    blk, eblk, m, own_v, e_v, tr_v,
    rblk, reb, rm, s1, sf, se, ms, mx, nz, ec, ef, s2, ry, re, rmy, rmx, rey, rz, rn, eag, rt,
    ia, ib, ie, ra, rg, ree,
    c_s, c_r, y_s, y_r, e_s, e_r, my_s, my_r, mx_s, mx_r, ey_s, ey_r, z_s, z_r, n_s, n_r, g_s, g_r, t_s, t_r,
    a_s, a_r, f_s, ig_s, ig_r, ie_s, ie_r,
):
    x, y, z, c = coords()
    h = lax.div(z, 8)
    z8 = lax.rem(z, 8)
    u = 2 * x + c
    z_near = z + 1 - 2 * lax.rem(z, 2)
    is_a = z8 == a_place(c)
    is_g = (z8 == u) & (h == c)
    other = dev(x, y, z, 1 - c)

    def at_z(k):
        return dev(x, y, lax.rem(z + k, NZ), c)

    def at_y(k):
        return dev(x, lax.rem(y + k, NY), z, c)

    def at_x(k):
        return dev(lax.rem(x + k, NX), y, z, c)

    barrier = pltpu.get_barrier_semaphore()
    pl.semaphore_signal(barrier, inc=1, device_id=other, device_id_type=MESH)

    def greet_xy(k):
        pl.semaphore_signal(barrier, inc=1, device_id=at_x(k), device_id_type=MESH)
        pl.semaphore_signal(barrier, inc=1, device_id=at_y(k), device_id_type=MESH)

    def greet_z(k):
        pl.semaphore_signal(barrier, inc=1, device_id=at_z(k), device_id_type=MESH)

    def greet_group(k):
        near = 8 * h + lax.rem(z8 + k, 8)
        pl.semaphore_signal(barrier, inc=1, device_id=dev(x, y, near, 1 - c), device_id_type=MESH)

    def greet_plane(k):
        pl.semaphore_signal(barrier, inc=1, device_id=dev(lax.rem(x + k, NX), y, z, 1 - c), device_id_type=MESH)

    loop(1, 4, greet_xy)
    loop(1, 16, greet_z)
    loop(1, 8, greet_group)
    def greet_near(k):
        xx = lax.rem(x + 1 + lax.div(k, 2), NX)
        pl.semaphore_signal(barrier, inc=1, device_id=dev(xx, y, z_near, lax.rem(k, 2)), device_id_type=MESH)

    loop(1, NX, greet_plane)
    loop(0, 6, greet_near)
    grams(acts, cot, emb, ids_row, blk, eblk, m)
    pl.semaphore_wait(barrier, 38)

    def core_chunk(i):
        k = (2, 1, 3, 0)[i]
        yy = lax.rem(y + k, NY)
        return send(blk.at[1 - c, yy], rblk.at[yy], c_s.at[i], c_r.at[i], other)

    e_core = send(eblk.at[1 - c], reb, c_s.at[4], c_r.at[4], other)
    m_core = send(m, rm, c_s.at[5], c_r.at[5], other)
    e_core.start()
    m_core.start()
    for i in range(4):
        core_chunk(i).start()

    def g_copy(k):
        cols = pl.ds(pl.multiple_of(lax.rem(x + k, NX) * 512, 512), 512)
        return send(gw.at[:, cols], rt.at[x], t_s.at[k], t_r.at[k], at_x(k))

    def g_start(k):
        g_copy(k).start()

    loop(1, NX, g_start)

    e_core.wait_recv()
    e_sum = eblk[c] + reb[...]
    for k in range(NZ):
        se[k] = e_sum[4 * k : 4 * k + 4]

    def e_copy(k):
        return send(se.at[lax.rem(z + k, NZ)], re.at[k], e_s.at[k], e_r.at[k], at_z(k))

    def e_start(k):
        e_copy(k).start()

    loop(1, NZ, e_start)
    m_core.wait_recv()
    for k in range(NY):
        ms[k] = m[k] + rm[k]

    def my_copy(k):
        return send(ms.at[lax.rem(y + k, NY)], rmy.at[k], my_s.at[k], my_r.at[k], at_y(k))

    def mx_copy(k):
        return send(mx, rmx.at[k], mx_s.at[k], mx_r.at[k], at_x(k))

    loop(1, NY, lambda k: my_copy(k).start())

    ahead, far, behind = lax.rem(y + 1, NY), lax.rem(y + 2, NY), lax.rem(y + 3, NY)
    low, high = pl.ds(0, 104), pl.ds(104, 96)

    def y_copy(i):
        src = (s1.at[far, low], s1.at[far, high], s1.at[ahead, high], s1.at[behind, low], sf.at[low], sf.at[high])[i]
        dst = (ry.at[0, low], ry.at[0, high], ry.at[1, high], ry.at[2, low], ry.at[1, low], ry.at[2, high])[i]
        return send(src, dst, y_s.at[i], y_r.at[i], at_y(3 if i % 2 else 1))

    for i in range(4):
        k = (2, 1, 3, 0)[i]
        core_chunk(i).wait_recv()
        yy = lax.rem(y + k, NY)
        s1[yy] = blk[c, yy] + rblk[yy]
        if i == 0:
            y_copy(0).start()
            y_copy(1).start()
        elif i < 3:
            y_copy(i + 1).start()
    y_copy(0).wait_recv()
    sf[0:104] = s1[ahead, 0:104] + ry[0, 0:104]
    y_copy(4).start()
    y_copy(1).wait_recv()
    sf[104:200] = s1[behind, 104:200] + ry[0, 104:200]
    y_copy(5).start()

    def my_add(k, total):
        my_copy(k).wait_recv()
        return total + rmy[k]

    mx[...] = lax.fori_loop(1, NY, my_add, ms[y])
    loop(1, NX, lambda k: mx_copy(k).start())

    for i in range(2, 6):
        y_copy(i).wait_recv()

    def z_copy(j):
        place = 8 * c + u if j == 2 else 8 * j + a_place(c)
        k = lax.rem(place - z + NZ, NZ)
        return k, send(s2.at[j], rz.at[k], z_s.at[j], z_r.at[k], dev(x, y, place, c))

    chunk = s1[y] + (ry[1] + ry[2])
    for j in range(3):
        s2[j, 0:64] = chunk[64 * j : 64 * j + 64]
        s2[j, 64:72] = jnp.broadcast_to(chunk[192 + j : 193 + j], (8, 128))
        k, copy = z_copy(j)

        @pl.when(k != 0)
        def _(copy=copy):
            copy.start()

    def e_add(k, total):
        e_copy(k).wait_recv()
        return total + re[k]

    ec[...] = lax.fori_loop(1, NZ, e_add, se[z])

    def ey_copy(k):
        return send(ec, rey.at[k], ey_s.at[k], ey_r.at[k], at_y(k))

    def ey_start(k):
        ey_copy(k).start()

    loop(1, NY, ey_start)

    def mx_add(k, total):
        mx_copy(k).wait_recv()
        return total + rmx[k]

    n = lax.fori_loop(1, NX, mx_add, mx[...])
    for k in range(NZ):
        half = k // 8
        nz[k] = jnp.concatenate([n[k : k + 1], n[16 + half : 17 + half], n[18 + half : 19 + half], n[20:21]], axis=0)

    def n_copy(k):
        return send(nz.at[lax.rem(z + k, NZ)], rn.at[k], n_s.at[k], n_r.at[k], at_z(k))

    def n_start(k):
        n_copy(k).start()

    loop(1, NZ, n_start)

    def ey_add(k, total):
        ey_copy(k).wait_recv()
        return total + rey[k]

    ef[...] = lax.fori_loop(1, NY, ey_add, ec[...])

    def g_out(k):
        return send(ef, eag.at[z], g_s.at[k], g_r.at[k], at_z(k))

    def g_out_start(k):
        g_out(k).start()

    loop(1, NZ, g_out_start)

    def n_add(k, total):
        n_copy(k).wait_recv()
        return total + rn[k]

    tr_v[...] = lax.fori_loop(1, NZ, n_add, nz[z])
    loop(1, NZ, lambda k: g_out(k).wait_recv())
    eag[z] = ef[...]
    for k in range(NZ):
        e_v[4 * k : 4 * k + 4] = eag[k]

    own_v[...] = s2[0]

    @pl.when(is_a | is_g)
    def _():
        def z_add(k, total):
            send(s2.at[0], rz.at[k], z_s.at[0], z_r.at[k], other).wait_recv()
            return total + rz[k]

        own_v[...] = lax.fori_loop(1, NZ, z_add, s2[jnp.where(is_a, h, 2)])

    ia[...], ib[...], ie[...] = inverses(own_v[...], e_v[...], tr_v[...])

    def a_copy(k, p):
        near = 8 * h + lax.rem(z8 + k, 8)
        return send((ia, ib)[p], ra.at[2 * c + p], a_s.at[8 * p + k], a_r.at[2 * c + p], dev(x, y, near, p))

    def a_side(p):
        return send((ia, ib)[p], ra.at[2 * c + p], a_s.at[8 * p], a_r.at[2 * c + p], other)

    def a_came(q):
        send(ia, ra.at[q], a_s.at[0], a_r.at[q], other).wait_recv()

    def a_pass(q):
        return send(ra.at[q], ra.at[q], f_s.at[q], a_r.at[q], other)

    def plane(k):
        v = lax.rem(u + k, 8)
        return dev(lax.div(v, 2), y, z, lax.rem(v, 2))

    def near_plane(k):
        return dev(lax.div(k, 2), y, z_near, lax.rem(k, 2))

    def ig_here(p, k):
        return send((ia, ib)[p], rg, ig_s.at[k], ig_r, plane(k))

    def ig_there(p, k):
        return send((ia, ib)[p], rg, ig_s.at[8 + k], ig_r, near_plane(k))

    def ie_copy(k):
        return send(ie, ree.at[u], ie_s.at[k], ie_r.at[k], plane(k))

    @pl.when(is_a)
    def _():
        for p in range(2):
            loop(1, 8, lambda k, p=p: a_copy(k, p).start())
        for p in range(2):
            a_side(p).start()
        ra[2 * c] = ia[...]
        ra[2 * c + 1] = ib[...]

    for p in range(2):

        @pl.when(is_g & (c == p))
        def _(p=p):
            loop(0, 8, lambda k: ig_there(1 - p, k).start())
            loop(1, 8, lambda k: ig_here(p, k).start())
            rg[...] = (ia, ib)[p][...]

    loop(1, 8, lambda k: ie_copy(k).start())
    ree[u] = ie[...]
    loop(1, NX, lambda k: g_copy(k).wait_recv())
    rt[x] = gw[:, pl.ds(pl.multiple_of(x * 512, 512), 512)]

    @pl.when(jnp.logical_not(is_g))
    def _():
        send(ia, rg, ig_s.at[0], ig_r, other).wait_recv()

    pair = rg[...]
    g_block = jnp.where(c == 0, pair[:, :HEAD], pair[:, HEAD:])
    tile = jnp.concatenate([rt[k] for k in range(NX)], axis=0)
    left = jnp.dot(g_block, tile, precision=HI, preferred_element_type=F32)
    for q in range(4):
        here = z8 == a_place(q // 2)

        @pl.when(jnp.logical_not(here) & (c == q % 2))
        def _(q=q):
            a_came(q)
            a_pass(q).start()

    loop(1, 8, lambda k: ie_copy(k).wait_recv())
    stats = tr_v[...]
    ratio_e = jnp.sqrt((TOKENS / VOCAB) / (trace_sums(stats)[3:4] / (TOKENS * WIDTH)))
    lane = lax.broadcasted_iota(jnp.int32, (16, 128), 1)
    row = lax.broadcasted_iota(jnp.int32, (16, 128), 0)
    picked = jnp.where(lane == row + (64 * c + 16 * x), jnp.broadcast_to(stats[0:1], (16, 128)), 0.0)
    row_scale = jnp.sum(picked, axis=1, keepdims=True) + DAMP * ratio_e
    for v in range(8):
        cols = slice(128 * v, 128 * v + 128)
        u_o[:, cols] = jnp.dot(ge[:, cols], blockdiag(ree[v]), precision=HI, preferred_element_type=F32) / row_scale
    for q in range(4):
        here = z8 == a_place(q // 2)

        @pl.when((here & (c != q // 2)) | (jnp.logical_not(here) & (c != q % 2)))
        def _(q=q):
            a_came(q)

        cols = slice(128 * q, 128 * q + 128)
        w_o[:, cols] = jnp.dot(left[:, cols], blockdiag(ra[q]), precision=HI, preferred_element_type=F32)

    @pl.when(is_a)
    def _():
        for p in range(2):
            loop(1, 8, lambda k, p=p: a_copy(k, p).wait_send())
            a_side(p).wait_send()

    for q in range(4):
        here = z8 == a_place(q // 2)

        @pl.when(jnp.logical_not(here) & (c == q % 2))
        def _(q=q):
            a_pass(q).wait_send()

    for p in range(2):

        @pl.when(is_g & (c == p))
        def _(p=p):
            loop(0, 8, lambda k: ig_there(1 - p, k).wait_send())
            loop(1, 8, lambda k: ig_here(p, k).wait_send())

    loop(1, 8, lambda k: ie_copy(k).wait_send())
    e_core.wait_send()
    m_core.wait_send()
    for i in range(4):
        core_chunk(i).wait_send()
    loop(1, NX, lambda k: g_copy(k).wait_send())
    loop(1, NZ, lambda k: e_copy(k).wait_send())
    loop(1, NY, lambda k: my_copy(k).wait_send())
    loop(1, NX, lambda k: mx_copy(k).wait_send())
    for i in range(6):
        y_copy(i).wait_send()
    loop(1, NY, lambda k: ey_copy(k).wait_send())
    loop(1, NZ, lambda k: n_copy(k).wait_send())
    loop(1, NZ, lambda k: g_out(k).wait_send())
    for j in range(3):
        k, copy = z_copy(j)

        @pl.when(k != 0)
        def _(copy=copy):
            copy.wait_send()


def finish_kernel(w, u, w_o, u_o):
    w_o[...] = w[...]
    u_o[...] = u[...]


def vmem(count):
    return [pl.BlockSpec(memory_space=pltpu.VMEM)] * count


def shape(*dims):
    return jax.ShapeDtypeStruct(dims, F32)


def local(acts, out_cot, emb_ids, emb_cot, grad_w, grad_e):
    dma = pltpu.SemaphoreType.DMA
    buffers = [
        (2, 4, 200, 128), (2, 64, 128), (4, 24, 128), (72, 128), (64, 128), (4, 128),
        (4, 200, 128), (64, 128), (4, 24, 128), (4, 200, 128), (200, 128), (16, 4, 128), (4, 24, 128), (24, 128),
        (16, 4, 128), (4, 128), (4, 128), (3, 72, 128), (3, 200, 128), (16, 4, 128),
        (4, 24, 128), (4, 24, 128), (4, 4, 128), (16, 72, 128), (16, 4, 128), (16, 4, 128), (4, 16, 512),
        (64, 128), (64, 128), (64, 128), (4, 64, 128), (64, 128), (8, 64, 128),
    ]
    update_w, update_e = pl.pallas_call(
        whole_kernel,
        out_shape=(shape(64, 512), shape(16, 1024)),
        in_specs=vmem(6),
        out_specs=tuple(vmem(2)),
        scratch_shapes=[pltpu.VMEM(dims, F32) for dims in buffers]
        + [dma((n,)) for n in (6, 6, 6, 6, 16, 16, 4, 4, 4, 4, 4, 4, 3, 16, 16, 16, 16, 16, 4, 4)]
        + [dma((16,)), dma((4,)), dma((4,)), dma((16,)), dma, dma((8,)), dma((8,))],
        compiler_params=pltpu.CompilerParams(collective_id=0, has_side_effects=True),
        name="whole",
    )(acts, out_cot, emb_cot, emb_ids.reshape(1, 64), grad_w, grad_e)
    return pl.pallas_call(
        finish_kernel,
        out_shape=(shape(64, 512), shape(16, 1024)),
        in_specs=vmem(2),
        out_specs=tuple(vmem(2)),
        name="finish",
    )(update_w, update_e)


def solution(mesh):
    in_specs = (
        P(None, "dp", "tensor"),
        P(None, "dp", "tensor"),
        P(("dp", "tensor")),
        P("dp", "tensor"),
        P(("dp", "tensor"), None),
        P(("dp", "tensor"), None),
    )
    out_specs = (P("dp", "tensor"), P(("dp", "tensor"), None))
    return jax.shard_map(local, mesh=mesh, in_specs=in_specs, out_specs=out_specs, check_vma=False)
```

```python
import jax
import jax.numpy as jnp
from jax import lax
from jax.experimental import pallas as pl
from jax.experimental.pallas import tpu as pltpu
from jax.sharding import PartitionSpec as P

HEAD = 64
NS_ITERS = 4
DAMP = 0.7
LAYERS = 8
TOKENS = 32768
VOCAB = 8192
WIDTH = 1024
INNER = 2048
NX, NY, NZ = 4, 4, 16
MESH = pl.DeviceIdType.MESH
F32 = jnp.float32
HI = lax.Precision.HIGHEST


def coords():
    d = lax.axis_index("dp").astype(jnp.int32)
    x = lax.axis_index("tensor").astype(jnp.int32)
    c = lax.rem(d, 2)
    z = lax.rem(lax.div(d, 2), NZ)
    y = lax.div(d, 2 * NZ)
    return x, y, z, c


def dev(x, y, z, c):
    return ((y * NZ + z) * 2 + c, x)


def a_place(core):
    return 3 + core


def send(src, dst, send_sem, recv_sem, device):
    return pltpu.make_async_remote_copy(
        src_ref=src, dst_ref=dst, send_sem=send_sem, recv_sem=recv_sem, device_id=device, device_id_type=MESH
    )


def loop(low, high, body):
    def step(k, carry):
        body(k)
        return carry

    lax.fori_loop(low, high, step, 0)


def pair_of(product):
    lane = lax.broadcasted_iota(jnp.int32, (HEAD, 2 * HEAD), 1)
    return jnp.where(lane < HEAD, product[:HEAD], product[HEAD:])


def blockdiag(pair):
    lane = lax.broadcasted_iota(jnp.int32, (HEAD, 2 * HEAD), 1)
    zero = jnp.zeros_like(pair)
    return jnp.concatenate([jnp.where(lane < HEAD, pair, zero), jnp.where(lane < HEAD, zero, pair)], axis=0)


def grams(acts, cot, emb, ids_row, blk, eblk, m, layers):
    lane = lax.broadcasted_iota(jnp.int32, (HEAD, 2 * HEAD), 1)
    row = lax.broadcasted_iota(jnp.int32, (HEAD, 2 * HEAD), 0)
    on_diag = (lane == row) | (lane == row + HEAD)

    def gram(x):
        full = lax.dot_general(x, x, (((0,), (0,)), ((), ())), preferred_element_type=F32)
        pair = pair_of(full)
        return pair, jnp.sum(jnp.where(on_diag, pair, 0.0), axis=0, keepdims=True)

    ids = ids_row[...]
    hit_row = (lax.broadcasted_iota(jnp.int32, (64, 64), 0) == lax.shift_right_logical(ids, 7)).astype(F32)
    hit_lane = (lax.broadcasted_iota(jnp.int32, (128, 64), 0) == (ids & 127)).astype(F32)
    hist = lax.dot_general(
        hit_row.astype(jnp.bfloat16),
        hit_lane.astype(jnp.bfloat16),
        (((1,), (1,)), ((), ())),
        preferred_element_type=F32,
    )
    sum_e = jnp.zeros((1, 128), F32)
    for core in range(2):
        pair, diag = gram(emb[:, 128 * core : 128 * core + 128])
        eblk[core] = pair
        sum_e = sum_e + diag
    rows = {}
    upper = row <= jnp.where(lane < HEAD, lane, lane - HEAD)
    below = {}
    for layer in range(LAYERS):
        y, odd = layer // 2, layer % 2
        layers[layer][0].wait()
        layers[layer][1].wait()
        sum_a = jnp.zeros((1, 128), F32)
        sum_g = jnp.zeros((1, 128), F32)
        for core in range(2):
            first, diag_first = gram(acts[layer, :, 256 * core : 256 * core + 128])
            second, diag_second = gram(acts[layer, :, 256 * core + 128 : 256 * core + 256])
            blk[core, y, 64 * odd : 64 * odd + 64] = jnp.where(upper, first, second)
            below[core, odd] = diag_second
            sum_a = sum_a + (diag_first + diag_second)
        first, diag_first = gram(cot[layer, :, 0:128])
        second, diag_second = gram(cot[layer, :, 128:256])
        blk[odd, y, 128:192] = jnp.where(upper, first, second)
        below[odd, 2] = diag_second
        sum_g = sum_g + (diag_first + diag_second)
        rows[layer] = (sum_a, sum_g)
        if odd:
            for core in range(2):
                diags = [below[core, 0], below[core, 1], below[core, 2], jnp.zeros((5, 128), F32)]
                blk[core, y, 192:200] = jnp.concatenate(diags, axis=0)
    for y in range(NY):
        m[y, 0:16] = hist[16 * y : 16 * y + 16]
        tail = [rows[2 * y][0], rows[2 * y + 1][0], rows[2 * y][1], rows[2 * y + 1][1], sum_e]
        m[y, 16:24] = jnp.concatenate(tail + [jnp.zeros((3, 128), F32)], axis=0)


def trace_sums(tr):
    return jnp.sum(tr, axis=1, keepdims=True)


def inverses(own, e, tr):
    x, y, z, c = coords()
    sums = trace_sums(tr)
    ta = sums[1:2]
    tg = sums[2:3]
    ratio = jnp.sqrt((ta / (TOKENS * INNER)) / (tg / (TOKENS * WIDTH)))
    ratio_e = jnp.sqrt((TOKENS / VOCAB) / (sums[3:4] / (TOKENS * WIDTH)))
    is_g = lax.rem(z, 8) == 2 * x + c
    shift = jnp.where(is_g, DAMP / ratio, DAMP * ratio)
    side = 2 * HEAD
    row = lax.broadcasted_iota(jnp.int32, (side, side), 0)
    lane = lax.broadcasted_iota(jnp.int32, (side, side), 1)
    eye = (row == lane).astype(F32)
    top = lax.broadcasted_iota(jnp.int32, (side, 1), 0) < HEAD

    def start(pair, amount):
        mat = blockdiag(pair) * (1.0 / TOKENS) + amount * eye
        sums = jnp.sum(jnp.abs(mat), axis=1, keepdims=True)
        bound = jnp.where(
            top,
            jnp.max(jnp.where(top, sums, 0.0), axis=0, keepdims=True),
            jnp.max(jnp.where(top, 0.0, sums), axis=0, keepdims=True),
        )
        return eye - mat / bound, bound

    def fold(mat):
        return mat[:HEAD] + mat[HEAD:]

    both = own[:HEAD]
    turned = fold(blockdiag(both).T)
    at = lax.broadcasted_iota(jnp.int32, (HEAD, side), 0)
    to = lax.broadcasted_iota(jnp.int32, (HEAD, side), 1)
    to = jnp.where(to < HEAD, to, to - HEAD)
    first = jnp.where(at <= to, both, turned)
    second = jnp.where(at > to, both, jnp.where(at == to, own[HEAD : HEAD + 1], turned))
    def times(left, right):
        return [jnp.dot(p, q, precision=HI, preferred_element_type=F32) for p, q in zip(left, right)]

    begun = [start(first, shift), start(second, shift), start(e, DAMP / ratio_e)]
    power = [rest for rest, _ in begun]
    product = [eye + rest for rest in power]
    for _ in range(NS_ITERS - 1):
        power = times(power, power)
        product = times(product, [eye + rest for rest in power])
    return [fold(result / bound) for result, (_, bound) in zip(product, begun)]


def whole_kernel(
    acts_h, cot_h, emb_h, ids_h, gw_h, ge_h, w_o, u_o,
    acts, cot, emb, ids_row, gw, ge,
    blk, eblk, m, own_v, e_v, tr_v,
    rblk, reb, rm, s1, sf, se, ms, mx, nz, ec, ef, s2, ry, re, rmy, rmx, rey, rz, rn, eag, rt,
    ia, ib, ie, ra, rg, ree,
    c_s, c_r, y_s, y_r, e_s, e_r, my_s, my_r, mx_s, mx_r, ey_s, ey_r, z_s, z_r, n_s, n_r, g_s, g_r, t_s, t_r,
    a_s, a_r, f_s, ig_s, ig_r, ie_s, ie_r, acts_s, cot_s, in_s,
):
    x, y, z, c = coords()
    h = lax.div(z, 8)
    z8 = lax.rem(z, 8)
    u = 2 * x + c
    z_near = z + 1 - 2 * lax.rem(z, 2)
    is_a = z8 == a_place(c)
    is_g = (z8 == u) & (h == c)
    other = dev(x, y, z, 1 - c)

    def at_z(k):
        return dev(x, y, lax.rem(z + k, NZ), c)

    def at_y(k):
        return dev(x, lax.rem(y + k, NY), z, c)

    def at_x(k):
        return dev(lax.rem(x + k, NX), y, z, c)

    small = [
        pltpu.make_async_copy(src, dst, in_s.at[i])
        for i, (src, dst) in enumerate([(emb_h, emb), (ids_h, ids_row), (gw_h, gw), (ge_h, ge)])
    ]
    small[0].start()
    small[1].start()
    layers = [
        (
            pltpu.make_async_copy(acts_h.at[l], acts.at[l], acts_s.at[l]),
            pltpu.make_async_copy(cot_h.at[l], cot.at[l], cot_s.at[l]),
        )
        for l in range(LAYERS)
    ]
    for first, second in layers:
        first.start()
        second.start()
    small[2].start()
    small[3].start()

    barrier = pltpu.get_barrier_semaphore()
    pl.semaphore_signal(barrier, inc=1, device_id=other, device_id_type=MESH)

    def greet_xy(k):
        pl.semaphore_signal(barrier, inc=1, device_id=at_x(k), device_id_type=MESH)
        pl.semaphore_signal(barrier, inc=1, device_id=at_y(k), device_id_type=MESH)

    def greet_z(k):
        pl.semaphore_signal(barrier, inc=1, device_id=at_z(k), device_id_type=MESH)

    def greet_group(k):
        near = 8 * h + lax.rem(z8 + k, 8)
        pl.semaphore_signal(barrier, inc=1, device_id=dev(x, y, near, 1 - c), device_id_type=MESH)

    def greet_plane(k):
        pl.semaphore_signal(barrier, inc=1, device_id=dev(lax.rem(x + k, NX), y, z, 1 - c), device_id_type=MESH)

    loop(1, 4, greet_xy)
    loop(1, 16, greet_z)
    loop(1, 8, greet_group)
    def greet_near(k):
        xx = lax.rem(x + 1 + lax.div(k, 2), NX)
        pl.semaphore_signal(barrier, inc=1, device_id=dev(xx, y, z_near, lax.rem(k, 2)), device_id_type=MESH)

    loop(1, NX, greet_plane)
    loop(0, 6, greet_near)
    small[0].wait()
    small[1].wait()
    grams(acts, cot, emb, ids_row, blk, eblk, m, layers)
    small[2].wait()
    small[3].wait()
    pl.semaphore_wait(barrier, 38)

    def core_chunk(i):
        k = (2, 1, 3, 0)[i]
        yy = lax.rem(y + k, NY)
        return send(blk.at[1 - c, yy], rblk.at[yy], c_s.at[i], c_r.at[i], other)

    e_core = send(eblk.at[1 - c], reb, c_s.at[4], c_r.at[4], other)
    m_core = send(m, rm, c_s.at[5], c_r.at[5], other)
    e_core.start()
    m_core.start()
    for i in range(4):
        core_chunk(i).start()

    def g_copy(k):
        cols = pl.ds(pl.multiple_of(lax.rem(x + k, NX) * 512, 512), 512)
        return send(gw.at[:, cols], rt.at[x], t_s.at[k], t_r.at[k], at_x(k))

    def g_start(k):
        g_copy(k).start()

    loop(1, NX, g_start)

    e_core.wait_recv()
    e_sum = eblk[c] + reb[...]
    for k in range(NZ):
        se[k] = e_sum[4 * k : 4 * k + 4]

    def e_copy(k):
        return send(se.at[lax.rem(z + k, NZ)], re.at[k], e_s.at[k], e_r.at[k], at_z(k))

    def e_start(k):
        e_copy(k).start()

    loop(1, NZ, e_start)
    m_core.wait_recv()
    for k in range(NY):
        ms[k] = m[k] + rm[k]

    def my_copy(k):
        return send(ms.at[lax.rem(y + k, NY)], rmy.at[k], my_s.at[k], my_r.at[k], at_y(k))

    def mx_copy(k):
        return send(mx, rmx.at[k], mx_s.at[k], mx_r.at[k], at_x(k))

    loop(1, NY, lambda k: my_copy(k).start())

    ahead, far, behind = lax.rem(y + 1, NY), lax.rem(y + 2, NY), lax.rem(y + 3, NY)
    low, high = pl.ds(0, 104), pl.ds(104, 96)

    def y_copy(i):
        src = (s1.at[far, low], s1.at[far, high], s1.at[ahead, high], s1.at[behind, low], sf.at[low], sf.at[high])[i]
        dst = (ry.at[0, low], ry.at[0, high], ry.at[1, high], ry.at[2, low], ry.at[1, low], ry.at[2, high])[i]
        return send(src, dst, y_s.at[i], y_r.at[i], at_y(3 if i % 2 else 1))

    for i in range(4):
        k = (2, 1, 3, 0)[i]
        core_chunk(i).wait_recv()
        yy = lax.rem(y + k, NY)
        s1[yy] = blk[c, yy] + rblk[yy]
        if i == 0:
            y_copy(0).start()
            y_copy(1).start()
        elif i < 3:
            y_copy(i + 1).start()
    y_copy(0).wait_recv()
    sf[0:104] = s1[ahead, 0:104] + ry[0, 0:104]
    y_copy(4).start()
    y_copy(1).wait_recv()
    sf[104:200] = s1[behind, 104:200] + ry[0, 104:200]
    y_copy(5).start()

    def my_add(k, total):
        my_copy(k).wait_recv()
        return total + rmy[k]

    mx[...] = lax.fori_loop(1, NY, my_add, ms[y])
    loop(1, NX, lambda k: mx_copy(k).start())

    for i in range(2, 6):
        y_copy(i).wait_recv()

    def z_copy(j):
        place = 8 * c + u if j == 2 else 8 * j + a_place(c)
        k = lax.rem(place - z + NZ, NZ)
        return k, send(s2.at[j], rz.at[k], z_s.at[j], z_r.at[k], dev(x, y, place, c))

    chunk = s1[y] + (ry[1] + ry[2])
    for j in range(3):
        s2[j, 0:64] = chunk[64 * j : 64 * j + 64]
        s2[j, 64:72] = jnp.broadcast_to(chunk[192 + j : 193 + j], (8, 128))
        k, copy = z_copy(j)

        @pl.when(k != 0)
        def _(copy=copy):
            copy.start()

    def e_add(k, total):
        e_copy(k).wait_recv()
        return total + re[k]

    ec[...] = lax.fori_loop(1, NZ, e_add, se[z])

    def ey_copy(k):
        return send(ec, rey.at[k], ey_s.at[k], ey_r.at[k], at_y(k))

    def ey_start(k):
        ey_copy(k).start()

    loop(1, NY, ey_start)

    def mx_add(k, total):
        mx_copy(k).wait_recv()
        return total + rmx[k]

    n = lax.fori_loop(1, NX, mx_add, mx[...])
    for k in range(NZ):
        half = k // 8
        nz[k] = jnp.concatenate([n[k : k + 1], n[16 + half : 17 + half], n[18 + half : 19 + half], n[20:21]], axis=0)

    def n_copy(k):
        return send(nz.at[lax.rem(z + k, NZ)], rn.at[k], n_s.at[k], n_r.at[k], at_z(k))

    def n_start(k):
        n_copy(k).start()

    loop(1, NZ, n_start)

    def ey_add(k, total):
        ey_copy(k).wait_recv()
        return total + rey[k]

    ef[...] = lax.fori_loop(1, NY, ey_add, ec[...])

    def g_out(k):
        return send(ef, eag.at[z], g_s.at[k], g_r.at[k], at_z(k))

    def g_out_start(k):
        g_out(k).start()

    loop(1, NZ, g_out_start)

    def n_add(k, total):
        n_copy(k).wait_recv()
        return total + rn[k]

    tr_v[...] = lax.fori_loop(1, NZ, n_add, nz[z])
    loop(1, NZ, lambda k: g_out(k).wait_recv())
    eag[z] = ef[...]
    for k in range(NZ):
        e_v[4 * k : 4 * k + 4] = eag[k]

    own_v[...] = s2[0]

    @pl.when(is_a | is_g)
    def _():
        def z_add(k, total):
            send(s2.at[0], rz.at[k], z_s.at[0], z_r.at[k], other).wait_recv()
            return total + rz[k]

        own_v[...] = lax.fori_loop(1, NZ, z_add, s2[jnp.where(is_a, h, 2)])

    ia[...], ib[...], ie[...] = inverses(own_v[...], e_v[...], tr_v[...])

    def a_copy(k, p):
        near = 8 * h + lax.rem(z8 + k, 8)
        return send((ia, ib)[p], ra.at[2 * c + p], a_s.at[8 * p + k], a_r.at[2 * c + p], dev(x, y, near, p))

    def a_side(p):
        return send((ia, ib)[p], ra.at[2 * c + p], a_s.at[8 * p], a_r.at[2 * c + p], other)

    def a_came(q):
        send(ia, ra.at[q], a_s.at[0], a_r.at[q], other).wait_recv()

    def a_pass(q):
        return send(ra.at[q], ra.at[q], f_s.at[q], a_r.at[q], other)

    def plane(k):
        v = lax.rem(u + k, 8)
        return dev(lax.div(v, 2), y, z, lax.rem(v, 2))

    def near_plane(k):
        return dev(lax.div(k, 2), y, z_near, lax.rem(k, 2))

    def ig_here(p, k):
        return send((ia, ib)[p], rg, ig_s.at[k], ig_r, plane(k))

    def ig_there(p, k):
        return send((ia, ib)[p], rg, ig_s.at[8 + k], ig_r, near_plane(k))

    def ie_copy(k):
        return send(ie, ree.at[u], ie_s.at[k], ie_r.at[k], plane(k))

    @pl.when(is_a)
    def _():
        for p in range(2):
            loop(1, 8, lambda k, p=p: a_copy(k, p).start())
        for p in range(2):
            a_side(p).start()
        ra[2 * c] = ia[...]
        ra[2 * c + 1] = ib[...]

    for p in range(2):

        @pl.when(is_g & (c == p))
        def _(p=p):
            loop(0, 8, lambda k: ig_there(1 - p, k).start())
            loop(1, 8, lambda k: ig_here(p, k).start())
            rg[...] = (ia, ib)[p][...]

    loop(1, 8, lambda k: ie_copy(k).start())
    ree[u] = ie[...]
    loop(1, NX, lambda k: g_copy(k).wait_recv())
    rt[x] = gw[:, pl.ds(pl.multiple_of(x * 512, 512), 512)]

    @pl.when(jnp.logical_not(is_g))
    def _():
        send(ia, rg, ig_s.at[0], ig_r, other).wait_recv()

    pair = rg[...]
    g_block = jnp.where(c == 0, pair[:, :HEAD], pair[:, HEAD:])
    tile = jnp.concatenate([rt[k] for k in range(NX)], axis=0)
    left = jnp.dot(g_block, tile, precision=HI, preferred_element_type=F32)
    for q in range(4):
        here = z8 == a_place(q // 2)

        @pl.when(jnp.logical_not(here) & (c == q % 2))
        def _(q=q):
            a_came(q)
            a_pass(q).start()

    loop(1, 8, lambda k: ie_copy(k).wait_recv())
    stats = tr_v[...]
    ratio_e = jnp.sqrt((TOKENS / VOCAB) / (trace_sums(stats)[3:4] / (TOKENS * WIDTH)))
    lane = lax.broadcasted_iota(jnp.int32, (16, 128), 1)
    row = lax.broadcasted_iota(jnp.int32, (16, 128), 0)
    picked = jnp.where(lane == row + (64 * c + 16 * x), jnp.broadcast_to(stats[0:1], (16, 128)), 0.0)
    row_scale = jnp.sum(picked, axis=1, keepdims=True) + DAMP * ratio_e
    for v in range(8):
        cols = slice(128 * v, 128 * v + 128)
        u_o[:, cols] = jnp.dot(ge[:, cols], blockdiag(ree[v]), precision=HI, preferred_element_type=F32) / row_scale
    for q in range(4):
        here = z8 == a_place(q // 2)

        @pl.when((here & (c != q // 2)) | (jnp.logical_not(here) & (c != q % 2)))
        def _(q=q):
            a_came(q)

        cols = slice(128 * q, 128 * q + 128)
        w_o[:, cols] = jnp.dot(left[:, cols], blockdiag(ra[q]), precision=HI, preferred_element_type=F32)

    @pl.when(is_a)
    def _():
        for p in range(2):
            loop(1, 8, lambda k, p=p: a_copy(k, p).wait_send())
            a_side(p).wait_send()

    for q in range(4):
        here = z8 == a_place(q // 2)

        @pl.when(jnp.logical_not(here) & (c == q % 2))
        def _(q=q):
            a_pass(q).wait_send()

    for p in range(2):

        @pl.when(is_g & (c == p))
        def _(p=p):
            loop(0, 8, lambda k: ig_there(1 - p, k).wait_send())
            loop(1, 8, lambda k: ig_here(p, k).wait_send())

    loop(1, 8, lambda k: ie_copy(k).wait_send())
    e_core.wait_send()
    m_core.wait_send()
    for i in range(4):
        core_chunk(i).wait_send()
    loop(1, NX, lambda k: g_copy(k).wait_send())
    loop(1, NZ, lambda k: e_copy(k).wait_send())
    loop(1, NY, lambda k: my_copy(k).wait_send())
    loop(1, NX, lambda k: mx_copy(k).wait_send())
    for i in range(6):
        y_copy(i).wait_send()
    loop(1, NY, lambda k: ey_copy(k).wait_send())
    loop(1, NZ, lambda k: n_copy(k).wait_send())
    loop(1, NZ, lambda k: g_out(k).wait_send())
    for j in range(3):
        k, copy = z_copy(j)

        @pl.when(k != 0)
        def _(copy=copy):
            copy.wait_send()


def finish_kernel(w, u, w_o, u_o):
    w_o[...] = w[...]
    u_o[...] = u[...]


def vmem(count):
    return [pl.BlockSpec(memory_space=pltpu.VMEM)] * count


def shape(*dims):
    return jax.ShapeDtypeStruct(dims, F32)


def local(acts, out_cot, emb_ids, emb_cot, grad_w, grad_e):
    dma = pltpu.SemaphoreType.DMA
    buffers = [
        (2, 4, 200, 128), (2, 64, 128), (4, 24, 128), (72, 128), (64, 128), (4, 128),
        (4, 200, 128), (64, 128), (4, 24, 128), (4, 200, 128), (200, 128), (16, 4, 128), (4, 24, 128), (24, 128),
        (16, 4, 128), (4, 128), (4, 128), (3, 72, 128), (3, 200, 128), (16, 4, 128),
        (4, 24, 128), (4, 24, 128), (4, 4, 128), (16, 72, 128), (16, 4, 128), (16, 4, 128), (4, 16, 512),
        (64, 128), (64, 128), (64, 128), (4, 64, 128), (64, 128), (8, 64, 128),
    ]
    update_w, update_e = pl.pallas_call(
        whole_kernel,
        out_shape=(shape(64, 512), shape(16, 1024)),
        in_specs=[pl.BlockSpec(memory_space=pl.ANY)] * 6,
        out_specs=tuple(vmem(2)),
        scratch_shapes=[
            pltpu.VMEM((8, 256, 512), jnp.bfloat16),
            pltpu.VMEM((8, 256, 256), jnp.bfloat16),
            pltpu.VMEM((256, 256), jnp.bfloat16),
            pltpu.VMEM((1, 64), jnp.int32),
            pltpu.VMEM((16, 2048), F32),
            pltpu.VMEM((16, 1024), F32),
        ]
        + [pltpu.VMEM(dims, F32) for dims in buffers]
        + [dma((n,)) for n in (6, 6, 6, 6, 16, 16, 4, 4, 4, 4, 4, 4, 3, 16, 16, 16, 16, 16, 4, 4)]
        + [dma((16,)), dma((4,)), dma((4,)), dma((16,)), dma, dma((8,)), dma((8,)), dma((8,)), dma((8,)), dma((4,))],
        compiler_params=pltpu.CompilerParams(collective_id=0, has_side_effects=True),
        name="whole",
    )(acts, out_cot, emb_cot, emb_ids.reshape(1, 64), grad_w, grad_e)
    return pl.pallas_call(
        finish_kernel,
        out_shape=(shape(64, 512), shape(16, 1024)),
        in_specs=vmem(2),
        out_specs=tuple(vmem(2)),
        name="finish",
    )(update_w, update_e)


def solution(mesh):
    in_specs = (
        P(None, "dp", "tensor"),
        P(None, "dp", "tensor"),
        P(("dp", "tensor")),
        P("dp", "tensor"),
        P(("dp", "tensor"), None),
        P(("dp", "tensor"), None),
    )
    out_specs = (P("dp", "tensor"), P(("dp", "tensor"), None))
    return jax.shard_map(local, mesh=mesh, in_specs=in_specs, out_specs=out_specs, check_vma=False)
```

```python
import jax
import jax.numpy as jnp
from jax import lax
from jax.experimental import pallas as pl
from jax.experimental.pallas import tpu as pltpu
from jax.sharding import PartitionSpec as P

HEAD = 64
NS_ITERS = 4
DAMP = 0.7
LAYERS = 8
TOKENS = 32768
VOCAB = 8192
WIDTH = 1024
INNER = 2048
NX, NY, NZ = 4, 4, 16
MESH = pl.DeviceIdType.MESH
F32 = jnp.float32
HI = lax.Precision.HIGHEST


def coords():
    d = lax.axis_index("dp").astype(jnp.int32)
    x = lax.axis_index("tensor").astype(jnp.int32)
    c = lax.rem(d, 2)
    z = lax.rem(lax.div(d, 2), NZ)
    y = lax.div(d, 2 * NZ)
    return x, y, z, c


def dev(x, y, z, c):
    return ((y * NZ + z) * 2 + c, x)


def a_place(core):
    return 3 + core


def send(src, dst, send_sem, recv_sem, device):
    return pltpu.make_async_remote_copy(
        src_ref=src, dst_ref=dst, send_sem=send_sem, recv_sem=recv_sem, device_id=device, device_id_type=MESH
    )


def loop(low, high, body):
    def step(k, carry):
        body(k)
        return carry

    lax.fori_loop(low, high, step, 0)


def pair_of(product):
    lane = lax.broadcasted_iota(jnp.int32, (HEAD, 2 * HEAD), 1)
    return jnp.where(lane < HEAD, product[:HEAD], product[HEAD:])


def blockdiag(pair):
    lane = lax.broadcasted_iota(jnp.int32, (HEAD, 2 * HEAD), 1)
    zero = jnp.zeros_like(pair)
    return jnp.concatenate([jnp.where(lane < HEAD, pair, zero), jnp.where(lane < HEAD, zero, pair)], axis=0)


def grams(acts, cot, emb, ids_row, blk, eblk, m, layers):
    lane = lax.broadcasted_iota(jnp.int32, (HEAD, 2 * HEAD), 1)
    row = lax.broadcasted_iota(jnp.int32, (HEAD, 2 * HEAD), 0)
    on_diag = (lane == row) | (lane == row + HEAD)

    def gram(x):
        full = lax.dot_general(x, x, (((0,), (0,)), ((), ())), preferred_element_type=F32)
        pair = pair_of(full)
        return pair, jnp.sum(jnp.where(on_diag, pair, 0.0), axis=0, keepdims=True)

    ids = ids_row[...]
    hit_row = (lax.broadcasted_iota(jnp.int32, (64, 64), 0) == lax.shift_right_logical(ids, 7)).astype(F32)
    hit_lane = (lax.broadcasted_iota(jnp.int32, (128, 64), 0) == (ids & 127)).astype(F32)
    hist = lax.dot_general(
        hit_row.astype(jnp.bfloat16),
        hit_lane.astype(jnp.bfloat16),
        (((1,), (1,)), ((), ())),
        preferred_element_type=F32,
    )
    sum_e = jnp.zeros((1, 128), F32)
    for core in range(2):
        pair, diag = gram(emb[:, 128 * core : 128 * core + 128])
        eblk[core] = pair
        sum_e = sum_e + diag
    rows = {}
    upper = row <= jnp.where(lane < HEAD, lane, lane - HEAD)
    below = {}
    for layer in range(LAYERS):
        y, odd = layer // 2, layer % 2
        layers[layer][0].wait()
        layers[layer][1].wait()
        sum_a = jnp.zeros((1, 128), F32)
        sum_g = jnp.zeros((1, 128), F32)
        for core in range(2):
            first, diag_first = gram(acts[layer, :, 256 * core : 256 * core + 128])
            second, diag_second = gram(acts[layer, :, 256 * core + 128 : 256 * core + 256])
            blk[core, y, 64 * odd : 64 * odd + 64] = jnp.where(upper, first, second)
            below[core, odd] = diag_second
            sum_a = sum_a + (diag_first + diag_second)
        first, diag_first = gram(cot[layer, :, 0:128])
        second, diag_second = gram(cot[layer, :, 128:256])
        blk[odd, y, 128:192] = jnp.where(upper, first, second)
        below[odd, 2] = diag_second
        sum_g = sum_g + (diag_first + diag_second)
        rows[layer] = (sum_a, sum_g)
        if odd:
            for core in range(2):
                diags = [below[core, 0], below[core, 1], below[core, 2], jnp.zeros((5, 128), F32)]
                blk[core, y, 192:200] = jnp.concatenate(diags, axis=0)
    for y in range(NY):
        m[y, 0:16] = hist[16 * y : 16 * y + 16]
        tail = [rows[2 * y][0], rows[2 * y + 1][0], rows[2 * y][1], rows[2 * y + 1][1], sum_e]
        m[y, 16:24] = jnp.concatenate(tail + [jnp.zeros((3, 128), F32)], axis=0)


def trace_sums(tr):
    return jnp.sum(tr, axis=1, keepdims=True)


def inverses(own, e, tr):
    x, y, z, c = coords()
    sums = trace_sums(tr)
    ta = sums[1:2]
    tg = sums[2:3]
    ratio = jnp.sqrt((ta / (TOKENS * INNER)) / (tg / (TOKENS * WIDTH)))
    ratio_e = jnp.sqrt((TOKENS / VOCAB) / (sums[3:4] / (TOKENS * WIDTH)))
    is_g = lax.rem(z, 8) == 2 * x + c
    shift = jnp.where(is_g, DAMP / ratio, DAMP * ratio)
    side = 2 * HEAD
    row = lax.broadcasted_iota(jnp.int32, (side, side), 0)
    lane = lax.broadcasted_iota(jnp.int32, (side, side), 1)
    eye = (row == lane).astype(F32)
    top = lax.broadcasted_iota(jnp.int32, (side, 1), 0) < HEAD

    def start(pair, amount):
        mat = blockdiag(pair) * (1.0 / TOKENS) + amount * eye
        sums = jnp.sum(jnp.abs(mat), axis=1, keepdims=True)
        bound = jnp.where(
            top,
            jnp.max(jnp.where(top, sums, 0.0), axis=0, keepdims=True),
            jnp.max(jnp.where(top, 0.0, sums), axis=0, keepdims=True),
        )
        return eye - mat / bound, bound

    def fold(mat):
        return mat[:HEAD] + mat[HEAD:]

    both = own[:HEAD]
    turned = fold(blockdiag(both).T)
    at = lax.broadcasted_iota(jnp.int32, (HEAD, side), 0)
    to = lax.broadcasted_iota(jnp.int32, (HEAD, side), 1)
    to = jnp.where(to < HEAD, to, to - HEAD)
    first = jnp.where(at <= to, both, turned)
    second = jnp.where(at > to, both, jnp.where(at == to, own[HEAD : HEAD + 1], turned))
    def times(left, right):
        return [jnp.dot(p, q, precision=HI, preferred_element_type=F32) for p, q in zip(left, right)]

    begun = [start(first, shift), start(second, shift), start(e, DAMP / ratio_e)]
    power = [rest for rest, _ in begun]
    product = [eye + rest for rest in power]
    for _ in range(NS_ITERS - 1):
        power = times(power, power)
        product = times(product, [eye + rest for rest in power])
    return [fold(result / bound) for result, (_, bound) in zip(product, begun)]


def whole_kernel(
    acts_h, cot_h, emb_h, ids_h, gw_h, ge_h, w_o, u_o,
    acts, cot, emb, ids_row, gw, ge,
    blk, eblk, m, own_v, e_v, tr_v,
    rblk, reb, rm, s1, sf, se, ms, mx, nz, ec, ef, s2, ry, re, rmy, rmx, rey, rz, rn, eag, rt,
    ia, ib, ie, ra, rg, ree,
    c_s, c_r, y_s, y_r, e_s, e_r, my_s, my_r, mx_s, mx_r, ey_s, ey_r, z_s, z_r, n_s, n_r, g_s, g_r, t_s, t_r,
    a_s, a_r, f_s, ig_s, ig_r, ie_s, ie_r, acts_s, cot_s, in_s,
):
    x, y, z, c = coords()
    h = lax.div(z, 8)
    z8 = lax.rem(z, 8)
    u = 2 * x + c
    z_near = z + 1 - 2 * lax.rem(z, 2)
    is_a = z8 == a_place(c)
    is_g = (z8 == u) & (h == c)
    other = dev(x, y, z, 1 - c)

    def at_z(k):
        return dev(x, y, lax.rem(z + k, NZ), c)

    def at_y(k):
        return dev(x, lax.rem(y + k, NY), z, c)

    def at_x(k):
        return dev(lax.rem(x + k, NX), y, z, c)

    small = [
        pltpu.make_async_copy(src, dst, in_s.at[i])
        for i, (src, dst) in enumerate([(emb_h, emb), (ids_h, ids_row), (gw_h, gw), (ge_h, ge)])
    ]
    small[0].start()
    small[1].start()
    layers = [
        (
            pltpu.make_async_copy(acts_h.at[l], acts.at[l], acts_s.at[l]),
            pltpu.make_async_copy(cot_h.at[l], cot.at[l], cot_s.at[l]),
        )
        for l in range(LAYERS)
    ]
    for first, second in layers:
        first.start()
        second.start()
    small[2].start()
    small[3].start()

    barrier = pltpu.get_barrier_semaphore()
    pl.semaphore_signal(barrier, inc=1, device_id=other, device_id_type=MESH)

    def greet_xy(k):
        pl.semaphore_signal(barrier, inc=1, device_id=at_x(k), device_id_type=MESH)
        pl.semaphore_signal(barrier, inc=1, device_id=at_y(k), device_id_type=MESH)

    def greet_z(k):
        pl.semaphore_signal(barrier, inc=1, device_id=at_z(k), device_id_type=MESH)

    def greet_group(k):
        near = 8 * h + lax.rem(z8 + k, 8)
        pl.semaphore_signal(barrier, inc=1, device_id=dev(x, y, near, 1 - c), device_id_type=MESH)

    def greet_near(k):
        near = dev(lax.rem(x + k, NX), y, z_near, c)
        pl.semaphore_signal(barrier, inc=1, device_id=near, device_id_type=MESH)

    loop(1, 4, greet_xy)
    loop(1, 16, greet_z)
    loop(1, 8, greet_group)
    loop(1, NX, greet_near)
    small[0].wait()
    small[1].wait()
    grams(acts, cot, emb, ids_row, blk, eblk, m, layers)
    small[2].wait()
    small[3].wait()
    pl.semaphore_wait(barrier, 32)

    def core_chunk(i):
        k = (2, 1, 3, 0)[i]
        yy = lax.rem(y + k, NY)
        return send(blk.at[1 - c, yy], rblk.at[yy], c_s.at[i], c_r.at[i], other)

    e_core = send(eblk.at[1 - c], reb, c_s.at[4], c_r.at[4], other)
    m_core = send(m, rm, c_s.at[5], c_r.at[5], other)
    e_core.start()
    m_core.start()
    for i in range(4):
        core_chunk(i).start()

    def g_copy(k):
        cols = pl.ds(pl.multiple_of(lax.rem(x + k, NX) * 512, 512), 512)
        return send(gw.at[:, cols], rt.at[x], t_s.at[k], t_r.at[k], at_x(k))

    def g_start(k):
        g_copy(k).start()

    loop(1, NX, g_start)

    e_core.wait_recv()
    e_sum = eblk[c] + reb[...]
    for k in range(NZ):
        se[k] = e_sum[4 * k : 4 * k + 4]

    def e_copy(k):
        return send(se.at[lax.rem(z + k, NZ)], re.at[k], e_s.at[k], e_r.at[k], at_z(k))

    def e_start(k):
        e_copy(k).start()

    loop(1, NZ, e_start)
    m_core.wait_recv()
    for k in range(NY):
        ms[k] = m[k] + rm[k]

    def my_copy(k):
        return send(ms.at[lax.rem(y + k, NY)], rmy.at[k], my_s.at[k], my_r.at[k], at_y(k))

    def mx_copy(k):
        return send(mx, rmx.at[k], mx_s.at[k], mx_r.at[k], at_x(k))

    loop(1, NY, lambda k: my_copy(k).start())

    ahead, far, behind = lax.rem(y + 1, NY), lax.rem(y + 2, NY), lax.rem(y + 3, NY)
    low, high = pl.ds(0, 104), pl.ds(104, 96)

    def y_copy(i):
        src = (s1.at[far, low], s1.at[far, high], s1.at[ahead, high], s1.at[behind, low], sf.at[low], sf.at[high])[i]
        dst = (ry.at[0, low], ry.at[0, high], ry.at[1, high], ry.at[2, low], ry.at[1, low], ry.at[2, high])[i]
        return send(src, dst, y_s.at[i], y_r.at[i], at_y(3 if i % 2 else 1))

    for i in range(4):
        k = (2, 1, 3, 0)[i]
        core_chunk(i).wait_recv()
        yy = lax.rem(y + k, NY)
        s1[yy] = blk[c, yy] + rblk[yy]
        if i == 0:
            y_copy(0).start()
            y_copy(1).start()
        elif i < 3:
            y_copy(i + 1).start()
    y_copy(0).wait_recv()
    sf[0:104] = s1[ahead, 0:104] + ry[0, 0:104]
    y_copy(4).start()
    y_copy(1).wait_recv()
    sf[104:200] = s1[behind, 104:200] + ry[0, 104:200]
    y_copy(5).start()

    def my_add(k, total):
        my_copy(k).wait_recv()
        return total + rmy[k]

    mx[...] = lax.fori_loop(1, NY, my_add, ms[y])
    loop(1, NX, lambda k: mx_copy(k).start())

    for i in range(2, 6):
        y_copy(i).wait_recv()

    def z_copy(j):
        place = 8 * c + u if j == 2 else 8 * j + a_place(c)
        k = lax.rem(place - z + NZ, NZ)
        return k, send(s2.at[j], rz.at[k], z_s.at[j], z_r.at[k], dev(x, y, place, c))

    chunk = s1[y] + (ry[1] + ry[2])
    for j in range(3):
        s2[j, 0:64] = chunk[64 * j : 64 * j + 64]
        s2[j, 64:72] = jnp.broadcast_to(chunk[192 + j : 193 + j], (8, 128))
        k, copy = z_copy(j)

        @pl.when(k != 0)
        def _(copy=copy):
            copy.start()

    def e_add(k, total):
        e_copy(k).wait_recv()
        return total + re[k]

    ec[...] = lax.fori_loop(1, NZ, e_add, se[z])

    def ey_copy(k):
        return send(ec, rey.at[k], ey_s.at[k], ey_r.at[k], at_y(k))

    def ey_start(k):
        ey_copy(k).start()

    loop(1, NY, ey_start)

    def mx_add(k, total):
        mx_copy(k).wait_recv()
        return total + rmx[k]

    n = lax.fori_loop(1, NX, mx_add, mx[...])
    for k in range(NZ):
        half = k // 8
        nz[k] = jnp.concatenate([n[k : k + 1], n[16 + half : 17 + half], n[18 + half : 19 + half], n[20:21]], axis=0)

    def n_copy(k):
        return send(nz.at[lax.rem(z + k, NZ)], rn.at[k], n_s.at[k], n_r.at[k], at_z(k))

    def n_start(k):
        n_copy(k).start()

    loop(1, NZ, n_start)

    def ey_add(k, total):
        ey_copy(k).wait_recv()
        return total + rey[k]

    ef[...] = lax.fori_loop(1, NY, ey_add, ec[...])

    def g_out(k):
        return send(ef, eag.at[z], g_s.at[k], g_r.at[k], at_z(k))

    def g_out_start(k):
        g_out(k).start()

    loop(1, NZ, g_out_start)

    def n_add(k, total):
        n_copy(k).wait_recv()
        return total + rn[k]

    tr_v[...] = lax.fori_loop(1, NZ, n_add, nz[z])
    loop(1, NZ, lambda k: g_out(k).wait_recv())
    eag[z] = ef[...]
    for k in range(NZ):
        e_v[4 * k : 4 * k + 4] = eag[k]

    own_v[...] = s2[0]

    @pl.when(is_a | is_g)
    def _():
        def z_add(k, total):
            send(s2.at[0], rz.at[k], z_s.at[0], z_r.at[k], other).wait_recv()
            return total + rz[k]

        own_v[...] = lax.fori_loop(1, NZ, z_add, s2[jnp.where(is_a, h, 2)])

    ia[...], ib[...], ie[...] = inverses(own_v[...], e_v[...], tr_v[...])

    def a_copy(k, p):
        near = 8 * h + lax.rem(z8 + k, 8)
        return send((ia, ib)[p], ra.at[2 * c + p], a_s.at[8 * p + k], a_r.at[2 * c + p], dev(x, y, near, p))

    def a_side(p):
        return send((ia, ib)[p], ra.at[2 * c + p], a_s.at[8 * p], a_r.at[2 * c + p], other)

    def a_came(q):
        send(ia, ra.at[q], a_s.at[0], a_r.at[q], other).wait_recv()

    def a_pass(q):
        return send(ra.at[q], ra.at[q], f_s.at[q], a_r.at[q], other)

    def ig_here(p, k):
        return send((ia, ib)[p], rg, ig_s.at[k], ig_r, at_x(k))

    def ig_there(p, k):
        return send((ia, ib)[p], rg, ig_s.at[4 + k], ig_r, dev(k, y, z_near, c))

    def ig_pass():
        return send(rg, rg, ig_s.at[0], ig_r, other)

    def ig_side(p):
        return send((ia, ib)[p], rg, ig_s.at[0], ig_r, other)

    def ie_copy(k):
        return send(ie, ree.at[u], ie_s.at[k], ie_r.at[u], at_x(k))

    def ie_side():
        return send(ie, ree.at[u], ie_s.at[0], ie_r.at[u], other)

    def ie_pass(k):
        v = 2 * lax.rem(x + k, NX) + c
        return send(ree.at[v], ree.at[v], ie_s.at[4 + k], ie_r.at[v], other)

    def ie_come(k):
        v = 2 * lax.rem(x + k, NX) + (1 - c)
        return send(ie, ree.at[v], ie_s.at[0], ie_r.at[v], other)

    @pl.when(is_a)
    def _():
        for p in range(2):
            loop(1, 8, lambda k, p=p: a_copy(k, p).start())
        for p in range(2):
            a_side(p).start()
        ra[2 * c] = ia[...]
        ra[2 * c + 1] = ib[...]

    for p in range(2):

        @pl.when(is_g & (c == p))
        def _(p=p):
            loop(0, NX, lambda k: ig_there(1 - p, k).start())
            loop(1, NX, lambda k: ig_here(p, k).start())
            ig_side(p).start()
            rg[...] = (ia, ib)[p][...]

    loop(1, NX, lambda k: ie_copy(k).start())
    ie_side().start()
    ree[u] = ie[...]
    loop(1, NX, lambda k: g_copy(k).wait_recv())
    rt[x] = gw[:, pl.ds(pl.multiple_of(x * 512, 512), 512)]

    def ie_forward(k):
        ie_pass(k).wait_recv()
        ie_pass(k).start()

    loop(1, NX, ie_forward)

    @pl.when((c == h) & jnp.logical_not(is_g))
    def _():
        ig_pass().wait_recv()
        ig_pass().start()

    for q in range(4):
        here = z8 == a_place(q // 2)

        @pl.when(jnp.logical_not(here) & (c == q % 2))
        def _(q=q):
            a_came(q)
            a_pass(q).start()

    loop(0, NX, lambda k: ie_come(k).wait_recv())
    stats = tr_v[...]
    ratio_e = jnp.sqrt((TOKENS / VOCAB) / (trace_sums(stats)[3:4] / (TOKENS * WIDTH)))
    lane = lax.broadcasted_iota(jnp.int32, (16, 128), 1)
    row = lax.broadcasted_iota(jnp.int32, (16, 128), 0)
    picked = jnp.where(lane == row + (64 * c + 16 * x), jnp.broadcast_to(stats[0:1], (16, 128)), 0.0)
    row_scale = jnp.sum(picked, axis=1, keepdims=True) + DAMP * ratio_e
    for v in range(8):
        cols = slice(128 * v, 128 * v + 128)
        u_o[:, cols] = jnp.dot(ge[:, cols], blockdiag(ree[v]), precision=HI, preferred_element_type=F32) / row_scale

    @pl.when(c != h)
    def _():
        ig_pass().wait_recv()

    pair = rg[...]
    g_block = jnp.where(c == 0, pair[:, :HEAD], pair[:, HEAD:])
    tile = jnp.concatenate([rt[k] for k in range(NX)], axis=0)
    left = jnp.dot(g_block, tile, precision=HI, preferred_element_type=F32)
    for q in range(4):
        here = z8 == a_place(q // 2)

        @pl.when((here & (c != q // 2)) | (jnp.logical_not(here) & (c != q % 2)))
        def _(q=q):
            a_came(q)

        cols = slice(128 * q, 128 * q + 128)
        w_o[:, cols] = jnp.dot(left[:, cols], blockdiag(ra[q]), precision=HI, preferred_element_type=F32)

    @pl.when(is_a)
    def _():
        for p in range(2):
            loop(1, 8, lambda k, p=p: a_copy(k, p).wait_send())
            a_side(p).wait_send()

    for q in range(4):
        here = z8 == a_place(q // 2)

        @pl.when(jnp.logical_not(here) & (c == q % 2))
        def _(q=q):
            a_pass(q).wait_send()

    for p in range(2):

        @pl.when(is_g & (c == p))
        def _(p=p):
            loop(0, NX, lambda k: ig_there(1 - p, k).wait_send())
            loop(1, NX, lambda k: ig_here(p, k).wait_send())
            ig_side(p).wait_send()

    @pl.when((c == h) & jnp.logical_not(is_g))
    def _():
        ig_pass().wait_send()

    loop(1, NX, lambda k: ie_copy(k).wait_send())
    ie_side().wait_send()
    loop(1, NX, lambda k: ie_pass(k).wait_send())
    e_core.wait_send()
    m_core.wait_send()
    for i in range(4):
        core_chunk(i).wait_send()
    loop(1, NX, lambda k: g_copy(k).wait_send())
    loop(1, NZ, lambda k: e_copy(k).wait_send())
    loop(1, NY, lambda k: my_copy(k).wait_send())
    loop(1, NX, lambda k: mx_copy(k).wait_send())
    for i in range(6):
        y_copy(i).wait_send()
    loop(1, NY, lambda k: ey_copy(k).wait_send())
    loop(1, NZ, lambda k: n_copy(k).wait_send())
    loop(1, NZ, lambda k: g_out(k).wait_send())
    for j in range(3):
        k, copy = z_copy(j)

        @pl.when(k != 0)
        def _(copy=copy):
            copy.wait_send()


def finish_kernel(w, u, w_o, u_o):
    w_o[...] = w[...]
    u_o[...] = u[...]


def vmem(count):
    return [pl.BlockSpec(memory_space=pltpu.VMEM)] * count


def shape(*dims):
    return jax.ShapeDtypeStruct(dims, F32)


def local(acts, out_cot, emb_ids, emb_cot, grad_w, grad_e):
    dma = pltpu.SemaphoreType.DMA
    buffers = [
        (2, 4, 200, 128), (2, 64, 128), (4, 24, 128), (72, 128), (64, 128), (4, 128),
        (4, 200, 128), (64, 128), (4, 24, 128), (4, 200, 128), (200, 128), (16, 4, 128), (4, 24, 128), (24, 128),
        (16, 4, 128), (4, 128), (4, 128), (3, 72, 128), (3, 200, 128), (16, 4, 128),
        (4, 24, 128), (4, 24, 128), (4, 4, 128), (16, 72, 128), (16, 4, 128), (16, 4, 128), (4, 16, 512),
        (64, 128), (64, 128), (64, 128), (4, 64, 128), (64, 128), (8, 64, 128),
    ]
    update_w, update_e = pl.pallas_call(
        whole_kernel,
        out_shape=(shape(64, 512), shape(16, 1024)),
        in_specs=[pl.BlockSpec(memory_space=pl.ANY)] * 6,
        out_specs=tuple(vmem(2)),
        scratch_shapes=[
            pltpu.VMEM((8, 256, 512), jnp.bfloat16),
            pltpu.VMEM((8, 256, 256), jnp.bfloat16),
            pltpu.VMEM((256, 256), jnp.bfloat16),
            pltpu.VMEM((1, 64), jnp.int32),
            pltpu.VMEM((16, 2048), F32),
            pltpu.VMEM((16, 1024), F32),
        ]
        + [pltpu.VMEM(dims, F32) for dims in buffers]
        + [dma((n,)) for n in (6, 6, 6, 6, 16, 16, 4, 4, 4, 4, 4, 4, 3, 16, 16, 16, 16, 16, 4, 4)]
        + [dma((16,)), dma((4,)), dma((4,)), dma((16,)), dma, dma((8,)), dma((8,)), dma((8,)), dma((8,)), dma((4,))],
        compiler_params=pltpu.CompilerParams(collective_id=0, has_side_effects=True),
        name="whole",
    )(acts, out_cot, emb_cot, emb_ids.reshape(1, 64), grad_w, grad_e)
    return pl.pallas_call(
        finish_kernel,
        out_shape=(shape(64, 512), shape(16, 1024)),
        in_specs=vmem(2),
        out_specs=tuple(vmem(2)),
        name="finish",
    )(update_w, update_e)


def solution(mesh):
    in_specs = (
        P(None, "dp", "tensor"),
        P(None, "dp", "tensor"),
        P(("dp", "tensor")),
        P("dp", "tensor"),
        P(("dp", "tensor"), None),
        P(("dp", "tensor"), None),
    )
    out_specs = (P("dp", "tensor"), P(("dp", "tensor"), None))
    return jax.shard_map(local, mesh=mesh, in_specs=in_specs, out_specs=out_specs, check_vma=False)
```

```python
import jax
import jax.numpy as jnp
from jax import lax
from jax.experimental import pallas as pl
from jax.experimental.pallas import tpu as pltpu
from jax.sharding import PartitionSpec as P

HEAD = 64
NS_ITERS = 4
DAMP = 0.7
LAYERS = 8
TOKENS = 32768
VOCAB = 8192
WIDTH = 1024
INNER = 2048
NX, NY, NZ = 4, 4, 16
MESH = pl.DeviceIdType.MESH
F32 = jnp.float32
HI = lax.Precision.HIGHEST


def coords():
    d = lax.axis_index("dp").astype(jnp.int32)
    x = lax.axis_index("tensor").astype(jnp.int32)
    c = lax.rem(d, 2)
    z = lax.rem(lax.div(d, 2), NZ)
    y = lax.div(d, 2 * NZ)
    return x, y, z, c


def dev(x, y, z, c):
    return ((y * NZ + z) * 2 + c, x)


def a_place(core):
    return 5 - 3 * core


def send(src, dst, send_sem, recv_sem, device):
    return pltpu.make_async_remote_copy(
        src_ref=src, dst_ref=dst, send_sem=send_sem, recv_sem=recv_sem, device_id=device, device_id_type=MESH
    )


def loop(low, high, body):
    def step(k, carry):
        body(k)
        return carry

    lax.fori_loop(low, high, step, 0)


def pair_of(product):
    lane = lax.broadcasted_iota(jnp.int32, (HEAD, 2 * HEAD), 1)
    return jnp.where(lane < HEAD, product[:HEAD], product[HEAD:])


def blockdiag(pair):
    lane = lax.broadcasted_iota(jnp.int32, (HEAD, 2 * HEAD), 1)
    zero = jnp.zeros_like(pair)
    return jnp.concatenate([jnp.where(lane < HEAD, pair, zero), jnp.where(lane < HEAD, zero, pair)], axis=0)


def grams(acts, cot, emb, ids_row, blk, eblk, m, layers):
    lane = lax.broadcasted_iota(jnp.int32, (HEAD, 2 * HEAD), 1)
    row = lax.broadcasted_iota(jnp.int32, (HEAD, 2 * HEAD), 0)
    on_diag = (lane == row) | (lane == row + HEAD)

    def gram(x):
        full = lax.dot_general(x, x, (((0,), (0,)), ((), ())), preferred_element_type=F32)
        pair = pair_of(full)
        return pair, jnp.sum(jnp.where(on_diag, pair, 0.0), axis=0, keepdims=True)

    ids = ids_row[...]
    hit_row = (lax.broadcasted_iota(jnp.int32, (64, 64), 0) == lax.shift_right_logical(ids, 7)).astype(F32)
    hit_lane = (lax.broadcasted_iota(jnp.int32, (128, 64), 0) == (ids & 127)).astype(F32)
    hist = lax.dot_general(
        hit_row.astype(jnp.bfloat16),
        hit_lane.astype(jnp.bfloat16),
        (((1,), (1,)), ((), ())),
        preferred_element_type=F32,
    )
    sum_e = jnp.zeros((1, 128), F32)
    for core in range(2):
        pair, diag = gram(emb[:, 128 * core : 128 * core + 128])
        eblk[core] = pair
        sum_e = sum_e + diag
    rows = {}
    upper = row <= jnp.where(lane < HEAD, lane, lane - HEAD)
    below = {}
    for layer in range(LAYERS):
        y, odd = layer // 2, layer % 2
        layers[layer][0].wait()
        layers[layer][1].wait()
        sum_a = jnp.zeros((1, 128), F32)
        sum_g = jnp.zeros((1, 128), F32)
        for core in range(2):
            first, diag_first = gram(acts[layer, :, 256 * core : 256 * core + 128])
            second, diag_second = gram(acts[layer, :, 256 * core + 128 : 256 * core + 256])
            blk[core, y, 64 * odd : 64 * odd + 64] = jnp.where(upper, first, second)
            below[core, odd] = diag_second
            sum_a = sum_a + (diag_first + diag_second)
        first, diag_first = gram(cot[layer, :, 0:128])
        second, diag_second = gram(cot[layer, :, 128:256])
        blk[odd, y, 128:192] = jnp.where(upper, first, second)
        below[odd, 2] = diag_second
        sum_g = sum_g + (diag_first + diag_second)
        rows[layer] = (sum_a, sum_g)
        if odd:
            for core in range(2):
                diags = [below[core, 0], below[core, 1], below[core, 2], jnp.zeros((5, 128), F32)]
                blk[core, y, 192:200] = jnp.concatenate(diags, axis=0)
    for y in range(NY):
        m[y, 0:16] = hist[16 * y : 16 * y + 16]
        tail = [rows[2 * y][0], rows[2 * y + 1][0], rows[2 * y][1], rows[2 * y + 1][1], sum_e]
        m[y, 16:24] = jnp.concatenate(tail + [jnp.zeros((3, 128), F32)], axis=0)


def trace_sums(tr):
    return jnp.sum(tr, axis=1, keepdims=True)


def inverses(own, e, tr):
    x, y, z, c = coords()
    sums = trace_sums(tr)
    ta = sums[1:2]
    tg = sums[2:3]
    ratio = jnp.sqrt((ta / (TOKENS * INNER)) / (tg / (TOKENS * WIDTH)))
    ratio_e = jnp.sqrt((TOKENS / VOCAB) / (sums[3:4] / (TOKENS * WIDTH)))
    is_g = lax.rem(z, 8) == 2 * x + c
    shift = jnp.where(is_g, DAMP / ratio, DAMP * ratio)
    side = 2 * HEAD
    row = lax.broadcasted_iota(jnp.int32, (side, side), 0)
    lane = lax.broadcasted_iota(jnp.int32, (side, side), 1)
    eye = (row == lane).astype(F32)
    top = lax.broadcasted_iota(jnp.int32, (side, 1), 0) < HEAD

    def start(pair, amount):
        mat = blockdiag(pair) * (1.0 / TOKENS) + amount * eye
        sums = jnp.sum(jnp.abs(mat), axis=1, keepdims=True)
        bound = jnp.where(
            top,
            jnp.max(jnp.where(top, sums, 0.0), axis=0, keepdims=True),
            jnp.max(jnp.where(top, 0.0, sums), axis=0, keepdims=True),
        )
        return eye - mat / bound, bound

    def fold(mat):
        return mat[:HEAD] + mat[HEAD:]

    both = own[:HEAD]
    turned = fold(blockdiag(both).T)
    at = lax.broadcasted_iota(jnp.int32, (HEAD, side), 0)
    to = lax.broadcasted_iota(jnp.int32, (HEAD, side), 1)
    to = jnp.where(to < HEAD, to, to - HEAD)
    first = jnp.where(at <= to, both, turned)
    second = jnp.where(at > to, both, jnp.where(at == to, own[HEAD : HEAD + 1], turned))
    def times(left, right):
        return [jnp.dot(p, q, precision=HI, preferred_element_type=F32) for p, q in zip(left, right)]

    begun = [start(first, shift), start(second, shift), start(e, DAMP / ratio_e)]
    power = [rest for rest, _ in begun]
    product = [eye + rest for rest in power]
    for _ in range(NS_ITERS - 1):
        power = times(power, power)
        product = times(product, [eye + rest for rest in power])
    return [fold(result / bound) for result, (_, bound) in zip(product, begun)]


def whole_kernel(
    acts_h, cot_h, emb_h, ids_h, gw_h, ge_h, w_o, u_o,
    acts, cot, emb, ids_row, gw, ge,
    blk, eblk, m, own_v, e_v, tr_v,
    rblk, reb, rm, s1, sf, se, ms, mx, nz, ec, ef, s2, ry, re, rmy, rmx, rey, rz, rn, eag, rt,
    ia, ib, ie, ra, rg, ree,
    c_s, c_r, y_s, y_r, e_s, e_r, my_s, my_r, mx_s, mx_r, ey_s, ey_r, z_s, z_r, n_s, n_r, g_s, g_r, t_s, t_r,
    a_s, a_r, f_s, ig_s, ig_r, ie_s, ie_r, acts_s, cot_s, in_s,
):
    x, y, z, c = coords()
    h = lax.div(z, 8)
    z8 = lax.rem(z, 8)
    u = 2 * x + c
    z_near = z + 1 - 2 * lax.rem(z, 2)
    is_a = z8 == a_place(c)
    is_g = (z8 == u) & (h == c)
    other = dev(x, y, z, 1 - c)

    def at_z(k):
        return dev(x, y, lax.rem(z + k, NZ), c)

    def at_y(k):
        return dev(x, lax.rem(y + k, NY), z, c)

    def at_x(k):
        return dev(lax.rem(x + k, NX), y, z, c)

    small = [
        pltpu.make_async_copy(src, dst, in_s.at[i])
        for i, (src, dst) in enumerate([(emb_h, emb), (ids_h, ids_row), (gw_h, gw), (ge_h, ge)])
    ]
    small[0].start()
    small[1].start()
    layers = [
        (
            pltpu.make_async_copy(acts_h.at[l], acts.at[l], acts_s.at[l]),
            pltpu.make_async_copy(cot_h.at[l], cot.at[l], cot_s.at[l]),
        )
        for l in range(LAYERS)
    ]
    for first, second in layers:
        first.start()
        second.start()
    small[2].start()
    small[3].start()

    barrier = pltpu.get_barrier_semaphore()
    pl.semaphore_signal(barrier, inc=1, device_id=other, device_id_type=MESH)

    def greet_xy(k):
        pl.semaphore_signal(barrier, inc=1, device_id=at_x(k), device_id_type=MESH)
        pl.semaphore_signal(barrier, inc=1, device_id=at_y(k), device_id_type=MESH)

    def greet_z(k):
        pl.semaphore_signal(barrier, inc=1, device_id=at_z(k), device_id_type=MESH)

    def greet_group(k):
        near = 8 * h + lax.rem(z8 + k, 8)
        pl.semaphore_signal(barrier, inc=1, device_id=dev(x, y, near, 1 - c), device_id_type=MESH)

    def greet_near(k):
        near = dev(lax.rem(x + k, NX), y, z_near, c)
        pl.semaphore_signal(barrier, inc=1, device_id=near, device_id_type=MESH)

    loop(1, 4, greet_xy)
    loop(1, 16, greet_z)
    loop(1, 8, greet_group)
    loop(1, NX, greet_near)
    small[0].wait()
    small[1].wait()
    grams(acts, cot, emb, ids_row, blk, eblk, m, layers)
    small[2].wait()
    small[3].wait()
    pl.semaphore_wait(barrier, 32)

    def core_chunk(i):
        k = (2, 1, 3, 0)[i]
        yy = lax.rem(y + k, NY)
        return send(blk.at[1 - c, yy], rblk.at[yy], c_s.at[i], c_r.at[i], other)

    e_core = send(eblk.at[1 - c], reb, c_s.at[4], c_r.at[4], other)
    m_core = send(m, rm, c_s.at[5], c_r.at[5], other)
    e_core.start()
    m_core.start()
    for i in range(4):
        core_chunk(i).start()

    def g_copy(k):
        cols = pl.ds(pl.multiple_of(lax.rem(x + k, NX) * 512, 512), 512)
        return send(gw.at[:, cols], rt.at[x], t_s.at[k], t_r.at[k], at_x(k))

    def g_start(k):
        g_copy(k).start()

    loop(1, NX, g_start)

    e_core.wait_recv()
    e_sum = eblk[c] + reb[...]
    for k in range(NZ):
        se[k] = e_sum[4 * k : 4 * k + 4]

    def e_copy(k):
        return send(se.at[lax.rem(z + k, NZ)], re.at[k], e_s.at[k], e_r.at[k], at_z(k))

    def e_start(k):
        e_copy(k).start()

    loop(1, NZ, e_start)
    m_core.wait_recv()
    for k in range(NY):
        ms[k] = m[k] + rm[k]

    def my_copy(k):
        return send(ms.at[lax.rem(y + k, NY)], rmy.at[k], my_s.at[k], my_r.at[k], at_y(k))

    def mx_copy(k):
        return send(mx, rmx.at[k], mx_s.at[k], mx_r.at[k], at_x(k))

    loop(1, NY, lambda k: my_copy(k).start())

    ahead, far, behind = lax.rem(y + 1, NY), lax.rem(y + 2, NY), lax.rem(y + 3, NY)
    low, high = pl.ds(0, 104), pl.ds(104, 96)

    def y_copy(i):
        src = (s1.at[far, low], s1.at[far, high], s1.at[ahead, high], s1.at[behind, low], sf.at[low], sf.at[high])[i]
        dst = (ry.at[0, low], ry.at[0, high], ry.at[1, high], ry.at[2, low], ry.at[1, low], ry.at[2, high])[i]
        return send(src, dst, y_s.at[i], y_r.at[i], at_y(3 if i % 2 else 1))

    for i in range(4):
        k = (2, 1, 3, 0)[i]
        core_chunk(i).wait_recv()
        yy = lax.rem(y + k, NY)
        s1[yy] = blk[c, yy] + rblk[yy]
        if i == 0:
            y_copy(0).start()
            y_copy(1).start()
        elif i < 3:
            y_copy(i + 1).start()
    y_copy(0).wait_recv()
    sf[0:104] = s1[ahead, 0:104] + ry[0, 0:104]
    y_copy(4).start()
    y_copy(1).wait_recv()
    sf[104:200] = s1[behind, 104:200] + ry[0, 104:200]
    y_copy(5).start()

    def my_add(k, total):
        my_copy(k).wait_recv()
        return total + rmy[k]

    mx[...] = lax.fori_loop(1, NY, my_add, ms[y])
    loop(1, NX, lambda k: mx_copy(k).start())

    for i in range(2, 6):
        y_copy(i).wait_recv()

    def z_copy(j):
        place = 8 * c + u if j == 2 else 8 * j + a_place(c)
        k = lax.rem(place - z + NZ, NZ)
        return k, send(s2.at[j], rz.at[k], z_s.at[j], z_r.at[k], dev(x, y, place, c))

    chunk = s1[y] + (ry[1] + ry[2])
    for j in range(3):
        s2[j, 0:64] = chunk[64 * j : 64 * j + 64]
        s2[j, 64:72] = jnp.broadcast_to(chunk[192 + j : 193 + j], (8, 128))
        k, copy = z_copy(j)

        @pl.when(k != 0)
        def _(copy=copy):
            copy.start()

    def e_add(k, total):
        e_copy(k).wait_recv()
        return total + re[k]

    ec[...] = lax.fori_loop(1, NZ, e_add, se[z])

    def ey_copy(k):
        return send(ec, rey.at[k], ey_s.at[k], ey_r.at[k], at_y(k))

    def ey_start(k):
        ey_copy(k).start()

    loop(1, NY, ey_start)

    def mx_add(k, total):
        mx_copy(k).wait_recv()
        return total + rmx[k]

    n = lax.fori_loop(1, NX, mx_add, mx[...])
    for k in range(NZ):
        half = k // 8
        nz[k] = jnp.concatenate([n[k : k + 1], n[16 + half : 17 + half], n[18 + half : 19 + half], n[20:21]], axis=0)

    def n_copy(k):
        return send(nz.at[lax.rem(z + k, NZ)], rn.at[k], n_s.at[k], n_r.at[k], at_z(k))

    def n_start(k):
        n_copy(k).start()

    loop(1, NZ, n_start)

    def ey_add(k, total):
        ey_copy(k).wait_recv()
        return total + rey[k]

    ef[...] = lax.fori_loop(1, NY, ey_add, ec[...])

    def g_out(k):
        return send(ef, eag.at[z], g_s.at[k], g_r.at[k], at_z(k))

    def g_out_start(k):
        g_out(k).start()

    loop(1, NZ, g_out_start)

    def n_add(k, total):
        n_copy(k).wait_recv()
        return total + rn[k]

    tr_v[...] = lax.fori_loop(1, NZ, n_add, nz[z])
    loop(1, NZ, lambda k: g_out(k).wait_recv())
    eag[z] = ef[...]
    for k in range(NZ):
        e_v[4 * k : 4 * k + 4] = eag[k]

    own_v[...] = s2[0]

    @pl.when(is_a | is_g)
    def _():
        def z_add(k, total):
            send(s2.at[0], rz.at[k], z_s.at[0], z_r.at[k], other).wait_recv()
            return total + rz[k]

        own_v[...] = lax.fori_loop(1, NZ, z_add, s2[jnp.where(is_a, h, 2)])

    ia[...], ib[...], ie[...] = inverses(own_v[...], e_v[...], tr_v[...])

    def a_copy(k, p):
        near = 8 * h + lax.rem(z8 + k, 8)
        return send((ia, ib)[p], ra.at[2 * c + p], a_s.at[8 * p + k], a_r.at[2 * c + p], dev(x, y, near, p))

    def a_side(p):
        return send((ia, ib)[p], ra.at[2 * c + p], a_s.at[8 * p], a_r.at[2 * c + p], other)

    def a_came(q):
        send(ia, ra.at[q], a_s.at[0], a_r.at[q], other).wait_recv()

    def a_pass(q):
        return send(ra.at[q], ra.at[q], f_s.at[q], a_r.at[q], other)

    def ig_here(p, k):
        return send((ia, ib)[p], rg, ig_s.at[k], ig_r, at_x(k))

    def ig_there(p, k):
        return send((ia, ib)[p], rg, ig_s.at[4 + k], ig_r, dev(k, y, z_near, c))

    def ig_pass():
        return send(rg, rg, ig_s.at[0], ig_r, other)

    def ig_side(p):
        return send((ia, ib)[p], rg, ig_s.at[0], ig_r, other)

    def ie_copy(k):
        return send(ie, ree.at[u], ie_s.at[k], ie_r.at[u], at_x(k))

    def ie_side():
        return send(ie, ree.at[u], ie_s.at[0], ie_r.at[u], other)

    def ie_pass(k):
        v = 2 * lax.rem(x + k, NX) + c
        return send(ree.at[v], ree.at[v], ie_s.at[4 + k], ie_r.at[v], other)

    def ie_come(k):
        v = 2 * lax.rem(x + k, NX) + (1 - c)
        return send(ie, ree.at[v], ie_s.at[0], ie_r.at[v], other)

    @pl.when(is_a)
    def _():
        for p in range(2):
            loop(1, 8, lambda k, p=p: a_copy(k, p).start())
        for p in range(2):
            a_side(p).start()
        ra[2 * c] = ia[...]
        ra[2 * c + 1] = ib[...]

    for p in range(2):

        @pl.when(is_g & (c == p))
        def _(p=p):
            loop(0, NX, lambda k: ig_there(1 - p, k).start())
            loop(1, NX, lambda k: ig_here(p, k).start())
            ig_side(p).start()
            rg[...] = (ia, ib)[p][...]

    loop(1, NX, lambda k: ie_copy(k).start())
    ie_side().start()
    ree[u] = ie[...]
    loop(1, NX, lambda k: g_copy(k).wait_recv())
    rt[x] = gw[:, pl.ds(pl.multiple_of(x * 512, 512), 512)]

    def ie_forward(k):
        ie_pass(k).wait_recv()
        ie_pass(k).start()

    loop(1, NX, ie_forward)

    @pl.when((c == h) & jnp.logical_not(is_g))
    def _():
        ig_pass().wait_recv()
        ig_pass().start()

    for q in range(4):
        here = z8 == a_place(q // 2)

        @pl.when(jnp.logical_not(here) & (c == q % 2))
        def _(q=q):
            a_came(q)
            a_pass(q).start()

    loop(0, NX, lambda k: ie_come(k).wait_recv())
    stats = tr_v[...]
    ratio_e = jnp.sqrt((TOKENS / VOCAB) / (trace_sums(stats)[3:4] / (TOKENS * WIDTH)))
    lane = lax.broadcasted_iota(jnp.int32, (16, 128), 1)
    row = lax.broadcasted_iota(jnp.int32, (16, 128), 0)
    picked = jnp.where(lane == row + (64 * c + 16 * x), jnp.broadcast_to(stats[0:1], (16, 128)), 0.0)
    row_scale = jnp.sum(picked, axis=1, keepdims=True) + DAMP * ratio_e
    for v in range(8):
        cols = slice(128 * v, 128 * v + 128)
        u_o[:, cols] = jnp.dot(ge[:, cols], blockdiag(ree[v]), precision=HI, preferred_element_type=F32) / row_scale

    @pl.when(c != h)
    def _():
        ig_pass().wait_recv()

    pair = rg[...]
    g_block = jnp.where(c == 0, pair[:, :HEAD], pair[:, HEAD:])
    tile = jnp.concatenate([rt[k] for k in range(NX)], axis=0)
    left = jnp.dot(g_block, tile, precision=HI, preferred_element_type=F32)
    for q in range(4):
        here = z8 == a_place(q // 2)

        @pl.when((here & (c != q // 2)) | (jnp.logical_not(here) & (c != q % 2)))
        def _(q=q):
            a_came(q)

        cols = slice(128 * q, 128 * q + 128)
        w_o[:, cols] = jnp.dot(left[:, cols], blockdiag(ra[q]), precision=HI, preferred_element_type=F32)

    @pl.when(is_a)
    def _():
        for p in range(2):
            loop(1, 8, lambda k, p=p: a_copy(k, p).wait_send())
            a_side(p).wait_send()

    for q in range(4):
        here = z8 == a_place(q // 2)

        @pl.when(jnp.logical_not(here) & (c == q % 2))
        def _(q=q):
            a_pass(q).wait_send()

    for p in range(2):

        @pl.when(is_g & (c == p))
        def _(p=p):
            loop(0, NX, lambda k: ig_there(1 - p, k).wait_send())
            loop(1, NX, lambda k: ig_here(p, k).wait_send())
            ig_side(p).wait_send()

    @pl.when((c == h) & jnp.logical_not(is_g))
    def _():
        ig_pass().wait_send()

    loop(1, NX, lambda k: ie_copy(k).wait_send())
    ie_side().wait_send()
    loop(1, NX, lambda k: ie_pass(k).wait_send())
    e_core.wait_send()
    m_core.wait_send()
    for i in range(4):
        core_chunk(i).wait_send()
    loop(1, NX, lambda k: g_copy(k).wait_send())
    loop(1, NZ, lambda k: e_copy(k).wait_send())
    loop(1, NY, lambda k: my_copy(k).wait_send())
    loop(1, NX, lambda k: mx_copy(k).wait_send())
    for i in range(6):
        y_copy(i).wait_send()
    loop(1, NY, lambda k: ey_copy(k).wait_send())
    loop(1, NZ, lambda k: n_copy(k).wait_send())
    loop(1, NZ, lambda k: g_out(k).wait_send())
    for j in range(3):
        k, copy = z_copy(j)

        @pl.when(k != 0)
        def _(copy=copy):
            copy.wait_send()


def finish_kernel(w, u, w_o, u_o):
    w_o[...] = w[...]
    u_o[...] = u[...]


def vmem(count):
    return [pl.BlockSpec(memory_space=pltpu.VMEM)] * count


def shape(*dims):
    return jax.ShapeDtypeStruct(dims, F32)


def local(acts, out_cot, emb_ids, emb_cot, grad_w, grad_e):
    dma = pltpu.SemaphoreType.DMA
    buffers = [
        (2, 4, 200, 128), (2, 64, 128), (4, 24, 128), (72, 128), (64, 128), (4, 128),
        (4, 200, 128), (64, 128), (4, 24, 128), (4, 200, 128), (200, 128), (16, 4, 128), (4, 24, 128), (24, 128),
        (16, 4, 128), (4, 128), (4, 128), (3, 72, 128), (3, 200, 128), (16, 4, 128),
        (4, 24, 128), (4, 24, 128), (4, 4, 128), (16, 72, 128), (16, 4, 128), (16, 4, 128), (4, 16, 512),
        (64, 128), (64, 128), (64, 128), (4, 64, 128), (64, 128), (8, 64, 128),
    ]
    update_w, update_e = pl.pallas_call(
        whole_kernel,
        out_shape=(shape(64, 512), shape(16, 1024)),
        in_specs=[pl.BlockSpec(memory_space=pl.ANY)] * 6,
        out_specs=tuple(vmem(2)),
        scratch_shapes=[
            pltpu.VMEM((8, 256, 512), jnp.bfloat16),
            pltpu.VMEM((8, 256, 256), jnp.bfloat16),
            pltpu.VMEM((256, 256), jnp.bfloat16),
            pltpu.VMEM((1, 64), jnp.int32),
            pltpu.VMEM((16, 2048), F32),
            pltpu.VMEM((16, 1024), F32),
        ]
        + [pltpu.VMEM(dims, F32) for dims in buffers]
        + [dma((n,)) for n in (6, 6, 6, 6, 16, 16, 4, 4, 4, 4, 4, 4, 3, 16, 16, 16, 16, 16, 4, 4)]
        + [dma((16,)), dma((4,)), dma((4,)), dma((16,)), dma, dma((8,)), dma((8,)), dma((8,)), dma((8,)), dma((4,))],
        compiler_params=pltpu.CompilerParams(collective_id=0, has_side_effects=True),
        name="whole",
    )(acts, out_cot, emb_cot, emb_ids.reshape(1, 64), grad_w, grad_e)
    return pl.pallas_call(
        finish_kernel,
        out_shape=(shape(64, 512), shape(16, 1024)),
        in_specs=vmem(2),
        out_specs=tuple(vmem(2)),
        name="finish",
    )(update_w, update_e)


def solution(mesh):
    in_specs = (
        P(None, "dp", "tensor"),
        P(None, "dp", "tensor"),
        P(("dp", "tensor")),
        P("dp", "tensor"),
        P(("dp", "tensor"), None),
        P(("dp", "tensor"), None),
    )
    out_specs = (P("dp", "tensor"), P(("dp", "tensor"), None))
    return jax.shard_map(local, mesh=mesh, in_specs=in_specs, out_specs=out_specs, check_vma=False)
```
